32 devices in a mesh: row: 16 (over z, x, core), col: 2 (over y).
Axes of the slice: x: 2, y: 2, z: 4, core: 2. Of those that a mesh axis runs over, the one named last changes fastest.
Arguments:
- tiles: bfloat16 [16, 2, 256, 128, 128], P('row', 'col'), may hold values from 0 to 0.00064849854
- tile_row: int32 [16, 2, 256], P('row', 'col'), may hold values from 0 to 16, as said below
- tile_col: int32 [16, 2, 256], P('row', 'col'), may hold values from 0 to 128, as said below
- right_vecs: bfloat16 [256, 32, 128], P(('row', 'col')), may hold values from -6 to 6
- left_vecs: bfloat16 [256, 32, 128], P(('row', 'col')), may hold values from -6 to 6
Outputs:
- right_next: float32 [256, 32, 128], P(('row', 'col'))
- left_next: float32 [256, 32, 128], P(('row', 'col'))
- gram: float32 [32, 32], replicated
The draws below stay inside these ranges and needn't reach their ends.
Inputs may be any that keep to these rules, and one draw needn't show every extreme that they name: Value 16 marks an empty slot; a slot is empty in tile_row exactly when it is empty in tile_col; live slots come first on each device; each device has 128 to 256 live slots and some device has all 256 live. `tile_col`: value 128 marks an empty slot, in the same slots as tile_row.
All inputs are finite; a program needn't handle non-finite values.
Results may differ from the reference program's by a relative error of at most 0.0003.
Values may be sent and summed in bfloat16 or wider, within the bound.
A program may use at most 64 MiB of HBM per device.

```python
import jax
import jax.numpy as jnp
from jax import lax

TILE = 128
K = 32
TRP = 8
RT = 16
CT = 128
NT = 256
NB = 32768
TMAX = 256
N_ROW = 16
N_COL = 2


def slot_pattern(key):
    base = jax.random.fold_in(key, 7)
    key_count, key_rows, key_cols, key_full = jax.random.split(base, 4)
    device_count = N_ROW * N_COL
    counts = TMAX // 2 + jax.random.randint(key_count, (device_count,), 0, TMAX // 2 + 1)
    full_device = jax.random.randint(key_full, (), 0, device_count)
    counts = jnp.where(jnp.arange(device_count) == full_device, TMAX, counts)
    live = jnp.arange(TMAX)[None, :] < counts[:, None]
    slot_rows = jax.random.randint(key_rows, (device_count, TMAX), 0, RT)
    slot_cols = jax.random.randint(key_cols, (device_count, TMAX), 0, CT)
    slot_rows = jnp.where(live, slot_rows, RT).reshape(N_ROW, N_COL, TMAX)
    slot_cols = jnp.where(live, slot_cols, CT).reshape(N_ROW, N_COL, TMAX)
    return (slot_rows.astype(jnp.int32), slot_cols.astype(jnp.int32))


def draw_tile_row(key, part):
    return slot_pattern(key)[0]


def draw_tile_col(key, part):
    return slot_pattern(key)[1]


def levels(stream_key, shape, pieces, least, top_value):
    factor_of = 1.0
    for axis_at, parts in pieces:
        heights = jax.random.uniform(jax.random.fold_in(jax.random.fold_in(stream_key, 6), axis_at), (parts,), jnp.float32, least / len(pieces), top_value / len(pieces))
        factor_of = factor_of * jnp.repeat(jnp.exp(heights), shape[axis_at] // parts).reshape((-1,) + (1,) * (len(shape) - 1 - axis_at))
    return factor_of


def gaussian(stream_key, shape, width, bound, pieces=(), held_as=jnp.bfloat16):
    result = width * jax.random.normal(stream_key, shape, jnp.float32)
    if pieces:
        result = result * levels(stream_key, shape, pieces, -0.22, 0.18)
    return jnp.clip(result, -bound, bound).astype(held_as)


def setup_inputs(seed: int = 0) -> dict:
    key_list = jax.random.split(jax.random.key(seed), 6)
    tiles = jnp.clip(0.00064849854 * jax.random.uniform(key_list[0], (N_ROW, N_COL, TMAX, TILE, TILE), jnp.float32) ** levels(key_list[0], (N_ROW, N_COL, TMAX, TILE, TILE), ((0, 16), (1, 2)), -0.2, 0.2), 0.0, 0.00064849854).astype(jnp.bfloat16)
    tile_row = draw_tile_row(jax.random.fold_in(key_list[5], 71), 0)
    tile_col = draw_tile_col(jax.random.fold_in(key_list[5], 71), 0)
    right_vecs = gaussian(key_list[3], (NT, K, TILE), 1.0, 6.0, ((0, 32),))
    left_vecs = gaussian(key_list[4], (NT, K, TILE), 1.0, 6.0, ((0, 32),))
    return dict(tiles=tiles, tile_row=tile_row, tile_col=tile_col, right_vecs=right_vecs, left_vecs=left_vecs)


def reference(tiles, tile_row, tile_col, right_vecs, left_vecs):
    highest = lax.Precision.HIGHEST
    row_block = jnp.arange(N_ROW, dtype=jnp.int32)[:, None, None]
    col_block = jnp.arange(N_COL, dtype=jnp.int32)[None, :, None]
    live = tile_row < RT
    global_rows = jnp.where(live, row_block * RT + tile_row, NT).astype(jnp.int32)
    global_cols = jnp.where(live, ((tile_col // TRP) * N_COL + col_block) * TRP + tile_col % TRP, NT).astype(jnp.int32)
    flat_tiles = tiles.reshape(N_ROW * N_COL, TMAX, TILE, TILE)
    flat_rows = global_rows.reshape(N_ROW * N_COL, TMAX)
    flat_cols = global_cols.reshape(N_ROW * N_COL, TMAX)
    right_float = right_vecs.astype(jnp.float32)
    left_float = left_vecs.astype(jnp.float32)

    def device_step(carry, item):
        image_right, image_left = carry
        tile_block, row_index, col_index = item
        tile_float = tile_block.astype(jnp.float32)
        right_in = jnp.take(right_float, jnp.minimum(col_index, NT - 1), axis=0)
        left_in = jnp.take(left_float, jnp.minimum(row_index, NT - 1), axis=0)
        forward = jnp.einsum("sef,skf->ske", tile_float, right_in, precision=highest)
        backward = jnp.einsum("sef,ske->skf", tile_float, left_in, precision=highest)
        image_right = image_right.at[row_index].add(forward, mode="drop")
        image_left = image_left.at[col_index].add(backward, mode="drop")
        return (image_right, image_left), None

    start = (jnp.zeros((NT, K, TILE), jnp.float32), jnp.zeros((NT, K, TILE), jnp.float32))
    (image_right, image_left), _ = lax.scan(device_step, start, (flat_tiles, flat_rows, flat_cols))
    gram = jnp.einsum("tke,tle->kl", left_float, image_right, precision=highest) * (NB ** -0.5)
    right_next = image_right - jnp.einsum("tke,kl->tle", right_float, gram, precision=highest)
    left_next = image_left - jnp.einsum("tle,kl->tke", left_float, gram, precision=highest)
    return right_next, left_next, gram
```

```python
import functools
from contextlib import nullcontext as scope

import jax
import jax.numpy as jnp
from jax import lax
from jax.experimental import pallas as pl
from jax.experimental.pallas import tpu as pltpu
from jax.sharding import PartitionSpec as P

MESH = pl.DeviceIdType.MESH
F32 = jnp.float32
BF16 = jnp.bfloat16
GROUP = 32
PAIR = 2
KGROUP = 8
TOP = 32767.0
LEAST = 2.0**-110
PAD = 1


def split(value):
    high = value.astype(BF16)
    low = (value - high.astype(F32)).astype(BF16)
    return high, low


def mul(a, b, dims=(((1,), (0,)), ((), ()))):
    return lax.dot_general(a, b, dims, preferred_element_type=F32)


def flip(at, d, size):
    total, bit = 0, 1
    while bit < size:
        digit = at // bit % 2
        total = total + bit * (1 - digit if d & bit else digit)
        bit *= 2
    return total


def kernel(
    sizes,
    row_at,
    col_at,
    right,
    left,
    tiles,
    out_y,
    out_z,
    out_g,
    tbuf,
    cv,
    rv,
    prod,
    zp,
    zc,
    zs,
    qx_out,
    sx_out,
    qx,
    sx,
    qz_out,
    sz_out,
    qz,
    sz,
    yp,
    qy_out,
    sy_out,
    qy,
    sy,
    ga,
    gb,
    row_s,
    col_s,
    row_v,
    col_v,
    own_sem,
    tile_sem,
    send_sem,
    left_sem,
    right_sem,
    zc_sem,
    zx_sem,
    sx_sem,
    zz_sem,
    sz_sem,
    zy_sem,
    sy_sem,
    g_sem,
):
    n_r, n_c, outer, inner, chunks = sizes
    piece, vecs, side = right.shape
    slots = tbuf.shape[0]
    step = slots // chunks
    block_rows = piece * n_c
    block_cols = piece * n_r
    wide = vecs + PAD
    part = piece * wide
    r = lax.axis_index("row")
    c = lax.axis_index("col")
    core = r % 2
    i = (r // 2) % inner
    o = r // (2 * inner)

    def row_of(oo, ii, cc):
        return (oo * inner + ii) * 2 + cc

    partner = (row_of(o, i, 1 - core), c)
    zs_of = [flip(o, d, outer) for d in range(outer)]
    xs_of = [flip(i, d, inner) for d in range(inner)]
    y_far = [(c + d) % n_c for d in range(1, n_c)]
    y_src = [(c - d + n_c) % n_c for d in range(1, n_c)]

    def tile_copy(ch):
        at = pl.ds(ch * step, step)
        return pltpu.make_async_copy(tiles.at[0, 0, at], tbuf.at[at], tile_sem.at[ch])

    own = [
        pltpu.make_async_copy(src, dst, own_sem.at[q])
        for q, (src, dst) in enumerate(
            [
                (right, cv.at[pl.ds(r * piece, piece)]),
                (left, rv.at[pl.ds(c * piece, piece)]),
                (row_at, row_s),
                (col_at, col_s),
                (row_at, row_v),
                (col_at, col_v),
            ]
        )
    ]
    for copy in own:
        copy.start()

    barrier = pltpu.get_barrier_semaphore()
    near = [
        ((i + d) % inner, (core + e) % 2, (i - d + inner) % inner)
        for d in range(inner)
        for e in range(2)
        if d or e
    ]
    wide_set = [
        ((o + d) % outer, (c + e) % n_c, (o - d + outer) % outer, (c - e + n_c) % n_c)
        for d in range(outer)
        for e in range(n_c)
        if d or e
    ]
    near_peers = [(row_of(o, x, cc), c) for x, cc, _ in near]
    near_src = [x * 2 + cc for _, cc, x in near]
    wide_peers = [(row_of(z, i, core), y) for z, y, _, _ in wide_set]
    wide_src = [z * n_c + y for _, _, z, y in wide_set]
    peers = near_peers + wide_peers
    for peer in peers:
        pl.semaphore_signal(barrier, inc=1, device_id=peer, device_id_type=MESH)
    pl.semaphore_wait(barrier, len(peers))

    sent = []

    def send(src, dst, sem, peer):
        copy = pltpu.make_async_remote_copy(
            src_ref=src,
            dst_ref=dst,
            send_sem=send_sem.at[len(sent)],
            recv_sem=sem,
            device_id=peer,
            device_id_type=MESH,
        )
        copy.start()
        sent.append(copy)

    def landed(ref, sem):
        pltpu.make_async_remote_copy(
            src_ref=ref,
            dst_ref=ref,
            send_sem=send_sem.at[0],
            recv_sem=sem,
            device_id=partner,
            device_id_type=MESH,
        ).wait_recv()

    def cv_at(rr):
        return cv.at[pl.ds(rr * piece, piece)]

    def rv_at(cc):
        return rv.at[pl.ds(cc * piece, piece)]

    for y in y_far:
        send(left, rv_at(c), left_sem.at[c], (r, y))
    for x in xs_of[1:]:
        send(right, cv_at(r), right_sem.at[r], (row_of(o, x, core), c))
    for z in zs_of[1:]:
        send(right, cv_at(r), right_sem.at[r], (row_of(z, i, core), c))
    send(right, cv_at(r), right_sem.at[r], partner)
    for ch in range(chunks):
        tile_copy(ch).start()

    def take_z(d):
        with scope("take_z%d" % d):
            got = row_of(zs_of[d], i, core)
            landed(cv_at(got), right_sem.at[got])
            for x in xs_of[1:]:
                send(cv_at(got), cv_at(got), right_sem.at[got], (row_of(o, x, core), c))
            send(cv_at(got), cv_at(got), right_sem.at[got], partner)

    def take_x(d):
        with scope("take_x%d" % d):
            for x in xs_of[1:]:
                got = row_of(zs_of[d], x, core)
                landed(cv_at(got), right_sem.at[got])
                send(cv_at(got), cv_at(got), right_sem.at[got], partner)

    def take_core(d):
        with scope("take_c%d" % d):
            for x in xs_of:
                got = row_of(zs_of[d], x, 1 - core)
                landed(cv_at(got), right_sem.at[got])

    def images(ch, vec_ref, index, limit, turned):
        def body(g, carry):
            for u in range(0, GROUP, PAIR):
                s = ch * step + g * GROUP + u
                xs = [vec_ref[jnp.minimum(index[0, s + q], limit - 1)] for q in range(PAIR)]
                ts = [tbuf[s + q] for q in range(PAIR)]
                dims = across if turned else plain
                got = mul(jnp.concatenate(xs, 0), jnp.concatenate(ts, 0 if turned else 1), dims)
                for q in range(PAIR):
                    block = got[q * vecs : (q + 1) * vecs, q * side : (q + 1) * side]
                    prod[pl.ds((s + q) * wide, vecs), :] = block
            return carry

        lax.fori_loop(0, step // GROUP, body, 0)

    plain = (((1,), (0,)), ((), ()))
    across = (((1,), (1,)), ((), ()))

    def gather_sums(index_v, rows, target, first=0, last=vecs // KGROUP):
        pick = lax.broadcasted_iota(jnp.int32, (rows, slots), 0) == index_v[...]
        pick = jnp.where(pick, 1.0, 0.0).astype(BF16)
        pick = jnp.concatenate([pick, pick], 1)

        def body(g, carry):
            for u in range(0, KGROUP, PAIR):
                k = g * KGROUP + u
                terms = [split(prod[pl.ds(k + q, slots, stride=wide), :]) for q in range(PAIR)]
                high = jnp.concatenate([t[0] for t in terms], 1)
                low = jnp.concatenate([t[1] for t in terms], 1)
                got = mul(pick, jnp.concatenate([high, low], 0))
                for q in range(PAIR):
                    block = got[:, q * side : (q + 1) * side]
                    target[pl.ds(k + q, rows, stride=wide), :] = block
            return carry

        lax.fori_loop(first, last, body, 0)

    def encode(block_of, q_ref, s_ref):
        scales = []
        for t in range(piece):
            block = block_of(t)
            top = jnp.maximum(jnp.max(jnp.abs(block), axis=0, keepdims=True), LEAST)
            q_ref[t * vecs : (t + 1) * vecs] = (
                jnp.round(block * (TOP / top)).astype(jnp.int32).astype(jnp.int16)
            )
            scales.append(top * (1.0 / TOP))
        s_ref[...] = jnp.concatenate(scales, 0)

    def decode(q_ref, s_ref, t):
        code = q_ref[t * vecs : (t + 1) * vecs].astype(jnp.int32).astype(F32)
        return code * s_ref[t : t + 1]

    def pair_sum(dz, dx, t):
        at = row_of(zs_of[dz], xs_of[dx], core) * part + t * wide
        return zp[pl.ds(at, vecs), :] + zc[dz * inner + dx, t * wide : t * wide + vecs]

    def give_core():
        with scope("give_core"):
            for dx in range(inner - 1, -1, -1):
                for dz in range(outer - 1, -1, -1):
                    at = pl.ds(row_of(zs_of[dz], xs_of[dx], 1 - core) * part, part)
                    slot = dz * inner + dx
                    send(zp.at[at], zc.at[slot], zc_sem.at[slot], partner)

    def give_x(dz):
        with scope("give_x%d" % dz):
            for dx in range(inner - 1, 0, -1):
                slot = dz * inner + dx
                landed(zc.at[slot], zc_sem.at[slot])
                out = qx_out.at[dx - 1, dz], sx_out.at[dx - 1, dz]
                encode(functools.partial(pair_sum, dz, dx), *out)
                peer = (row_of(o, xs_of[dx], core), c)
                send(out[0], qx.at[dx - 1, dz], zx_sem.at[dx - 1, dz], peer)
                send(out[1], sx.at[dx - 1, dz], sx_sem.at[dx - 1, dz], peer)

    def own_x():
        with scope("own_x"):
            for dz in range(outer - 1, -1, -1):
                landed(zc.at[dz * inner], zc_sem.at[dz * inner])

    def plane_sum(dz, t):
        total = pair_sum(dz, 0, t)
        for d in range(1, inner):
            total = total + decode(qx.at[d - 1, dz], sx.at[d - 1, dz], t)
        return total

    def give_z(dz):
        with scope("give_z%d" % dz):
            for d in range(1, inner):
                landed(qx.at[d - 1, dz], zx_sem.at[d - 1, dz])
                landed(sx.at[d - 1, dz], sx_sem.at[d - 1, dz])
            if dz:
                out = qz_out.at[dz - 1], sz_out.at[dz - 1]
                encode(functools.partial(plane_sum, dz), *out)
                peer = (row_of(zs_of[dz], i, core), c)
                send(out[0], qz.at[dz - 1], zz_sem.at[dz - 1], peer)
                send(out[1], sz.at[dz - 1], sz_sem.at[dz - 1], peer)
            else:
                for t in range(piece):
                    zs[t * vecs : (t + 1) * vecs] = plane_sum(0, t)

    def gram_plane(d, total):
        with scope("gram%d" % d):
            sums, mates = [], []
            for dx in range(inner):
                p = row_of(zs_of[d], xs_of[dx], core)
                for t in range(piece):
                    high, low = split(pair_sum(d, dx, t))
                    sums.append(jnp.concatenate([high, low], 0))
                    mates.append(cv[p * piece + t])
            return total + mul(jnp.concatenate(sums, 1), jnp.concatenate(mates, 1), across)

    def spread(value, buf, base, me, far):
        with scope("spread%d" % base):
            buf[me] = value
            for peer in far:
                send(buf.at[me], buf.at[me], g_sem.at[base + me], peer)

    def collect(buf, base, src):
        with scope("collect%d" % base):
            for q in src:
                landed(buf.at[q], g_sem.at[base + q])
            total = buf[0]
            for q in range(1, buf.shape[0]):
                total = total + buf[q]
            return total

    with scope("wait_left"):
        for copy in own:
            copy.wait()
        for y in y_src:
            landed(rv_at(y), left_sem.at[y])

    def left_images(first, last):
        with scope("imgL%d" % first):
            for ch in range(first, last):
                tile_copy(ch).wait()
                images(ch, rv, row_s, block_rows, False)

    def right_images(first, last):
        with scope("imgR%d" % first):
            for ch in range(first, last):
                images(ch, cv, col_s, block_cols, True)

    later = list(range(1, outer))
    groups = vecs // KGROUP
    left_images(0, 3)
    take_z(1)
    take_x(0)
    left_images(3, 6)
    for d in later[1:-1]:
        take_z(d)
    left_images(6, chunks)
    take_z(later[-1])
    with scope("gatherZ"):
        gather_sums(col_v, block_cols, zp)
    give_core()
    take_x(1)
    for d in later[::-1]:
        give_x(d)
    give_x(0)
    own_x()
    total = gram_plane(0, jnp.zeros((2 * vecs, vecs), F32))
    total = gram_plane(1, total)
    for d in later[1:]:
        take_x(d)
        total = gram_plane(d, total)
    spread(total[:vecs] + total[vecs:], gb, 2 * inner, o * n_c + c, wide_peers)
    for d in range(outer):
        take_core(d)

    right_images(0, 2)
    give_z(later[-1])
    right_images(2, 4)
    for d in later[-2:0:-1]:
        give_z(d)
    right_images(4, 6)
    give_z(later[0])
    right_images(6, chunks)
    with scope("gatherY"):
        gather_sums(row_v, block_rows, yp)
    with scope("give_y"):
        for d, y in enumerate(y_far):
            encode(lambda t: yp[pl.ds(y * part + t * wide, vecs), :], qy_out.at[d], sy_out.at[d])
            send(qy_out.at[d], qy.at[d], zy_sem.at[d], (r, y))
            send(sy_out.at[d], sy.at[d], sy_sem.at[d], (r, y))
    give_z(0)
    spread(collect(gb, 2 * inner, wide_src), ga, 0, i * 2 + core, near_peers)
    gram = collect(ga, 0, near_src)
    gram = gram * (block_cols * n_c * side) ** (-0.5)
    out_g[...] = gram
    with scope("wait_y"):
        for d in range(n_c - 1):
            landed(qy.at[d], zy_sem.at[d])
            landed(sy.at[d], sy_sem.at[d])
    with scope("out_y"):
        for t in range(piece):
            total = yp[pl.ds(c * part + t * wide, vecs), :]
            for d in range(n_c - 1):
                total = total + decode(qy.at[d], sy.at[d], t)
            out_y[t] = total
    with scope("wait_z"):
        for d in range(1, outer):
            landed(qz.at[d - 1], zz_sem.at[d - 1])
            landed(sz.at[d - 1], sz_sem.at[d - 1])
    with scope("out_z"):
        for t in range(piece):
            total = zs[t * vecs : (t + 1) * vecs]
            for d in range(1, outer):
                total = total + decode(qz.at[d - 1], sz.at[d - 1], t)
            out_z[t] = total
    with scope("wait_send"):
        for copy in sent:
            copy.wait_send()


def finish(y_ref, z_ref, gram_ref, right, left, out_r, out_l, out_g):
    piece, vecs, _ = right.shape
    gram = gram_ref[...]
    out_g[...] = gram
    high, low = split(gram)
    turned_high, turned_low = split(gram.T)
    for t in range(piece):
        out_r[t] = y_ref[t] - (mul(turned_high, right[t]) + mul(turned_low, right[t]))
        out_l[t] = z_ref[t] - (mul(high, left[t]) + mul(low, left[t]))


def solution(mesh):
    n_r, n_c = mesh.shape["row"], mesh.shape["col"]
    half = n_r // 2
    inner = 1 << ((half.bit_length() - 1) // 2)
    outer = half // inner

    def per_device(tiles, tile_row, tile_col, right_vecs, left_vecs):
        slots, side = tiles.shape[2], tiles.shape[3]
        piece, vecs, _ = right_vecs.shape
        chunks = 8
        wide = vecs + PAD
        part = piece * wide
        block_rows, block_cols = piece * n_c, piece * n_r
        planes = outer * inner
        near, far, mates = max(inner - 1, 1), max(outer - 1, 1), max(n_c - 1, 1)
        sends = (
            3 * (n_c - 1)
            + (outer - 1)
            + (inner - 1)
            + 1
            + (outer - 1) * inner
            + outer * (inner - 1)
            + planes
            + 2 * outer * (inner - 1)
            + 2 * (outer - 1)
            + (2 * inner - 1)
            + (outer * n_c - 1)
        )
        vmem = pl.BlockSpec(memory_space=pltpu.VMEM)
        dma = pltpu.SemaphoreType.DMA
        y_total, z_total, gram = pl.pallas_call(
            functools.partial(kernel, (n_r, n_c, outer, inner, chunks)),
            out_shape=(
                jax.ShapeDtypeStruct((piece, vecs, side), F32),
                jax.ShapeDtypeStruct((piece, vecs, side), F32),
                jax.ShapeDtypeStruct((vecs, vecs), F32),
            ),
            in_specs=[pl.BlockSpec(memory_space=pl.ANY)] * 5,
            out_specs=(vmem, vmem, vmem),
            scratch_shapes=[
                pltpu.VMEM((slots, side, side), BF16),
                pltpu.VMEM((block_cols, vecs, side), BF16),
                pltpu.VMEM((block_rows, vecs, side), BF16),
                pltpu.VMEM((slots * wide, side), F32),
                pltpu.VMEM((block_cols * wide, side), F32),
                pltpu.VMEM((planes, part, side), F32),
                pltpu.VMEM((piece * vecs, side), F32),
                *[
                    pltpu.VMEM(lead + shape, kind)
                    for lead in [(near, outer)] * 2 + [(far,)] * 2
                    for shape, kind in [((piece * vecs, side), jnp.int16), ((piece, side), F32)]
                ],
                pltpu.VMEM((block_rows * wide, side), F32),
                *[
                    pltpu.VMEM((mates,) + shape, kind)
                    for shape, kind in [((piece * vecs, side), jnp.int16), ((piece, side), F32)] * 2
                ],
                pltpu.VMEM((2 * inner, vecs, vecs), F32),
                pltpu.VMEM((outer * n_c, vecs, vecs), F32),
                *[pltpu.SMEM((1, slots), jnp.int32)] * 2,
                *[pltpu.VMEM((1, slots), jnp.int32)] * 2,
                dma((6,)),
                dma((chunks,)),
                dma((sends,)),
                dma((n_c,)),
                dma((n_r,)),
                dma((planes,)),
                *[dma((near, outer))] * 2,
                *[dma((far,))] * 2,
                *[dma((mates,))] * 2,
                dma((2 * inner + outer * n_c,)),
            ],
            compiler_params=pltpu.CompilerParams(
                collective_id=0, has_side_effects=True, vmem_limit_bytes=60 * 1024 * 1024
            ),
            name="arnoldi_step",
        )(tile_row.reshape(1, slots), tile_col.reshape(1, slots), right_vecs, left_vecs, tiles)
        return pl.pallas_call(
            finish,
            out_shape=(
                jax.ShapeDtypeStruct((piece, vecs, side), F32),
                jax.ShapeDtypeStruct((piece, vecs, side), F32),
                jax.ShapeDtypeStruct((vecs, vecs), F32),
            ),
            in_specs=[vmem] * 5,
            out_specs=(vmem, vmem, vmem),
            name="finish",
        )(y_total, z_total, gram, right_vecs, left_vecs)

    placed = (
        P("row", "col", None, None, None),
        P("row", "col", None),
        P("row", "col", None),
        P(("row", "col"), None, None),
        P(("row", "col"), None, None),
    )
    return jax.shard_map(
        per_device,
        mesh=mesh,
        in_specs=placed,
        out_specs=(P(("row", "col"), None, None), P(("row", "col"), None, None), P()),
        check_vma=False,
    )
```

```python
import functools
from contextlib import nullcontext as scope

import jax
import jax.numpy as jnp
from jax import lax
from jax.experimental import pallas as pl
from jax.experimental.pallas import tpu as pltpu
from jax.sharding import PartitionSpec as P

MESH = pl.DeviceIdType.MESH
F32 = jnp.float32
BF16 = jnp.bfloat16
GROUP = 32
PAIR = 2
KGROUP = 8
TOP = 32767.0
LEAST = 2.0**-110
PAD = 1


def split(value):
    high = value.astype(BF16)
    low = (value - high.astype(F32)).astype(BF16)
    return high, low


def mul(a, b, dims=(((1,), (0,)), ((), ()))):
    return lax.dot_general(a, b, dims, preferred_element_type=F32)


def flip(at, d, size):
    total, bit = 0, 1
    while bit < size:
        digit = at // bit % 2
        total = total + bit * (1 - digit if d & bit else digit)
        bit *= 2
    return total


def kernel(
    sizes,
    row_at,
    col_at,
    right,
    left,
    tiles,
    out_y,
    out_z,
    out_g,
    tbuf,
    cv,
    rv,
    prod,
    zp,
    zc,
    zs,
    qx_out,
    sx_out,
    qx,
    sx,
    qz_out,
    sz_out,
    qz,
    sz,
    yp,
    qy_out,
    sy_out,
    qy,
    sy,
    ga,
    gb,
    row_s,
    col_s,
    row_v,
    col_v,
    own_sem,
    tile_sem,
    send_sem,
    left_sem,
    right_sem,
    zc_sem,
    zx_sem,
    sx_sem,
    zz_sem,
    sz_sem,
    zy_sem,
    sy_sem,
    g_sem,
):
    n_r, n_c, outer, inner, chunks = sizes
    piece, vecs, side = right.shape
    slots = tbuf.shape[0]
    step = slots // chunks
    block_rows = piece * n_c
    block_cols = piece * n_r
    wide = vecs + PAD
    part = piece * wide
    r = lax.axis_index("row")
    c = lax.axis_index("col")
    core = r % 2
    i = (r // 2) % inner
    o = r // (2 * inner)

    def row_of(oo, ii, cc):
        return (oo * inner + ii) * 2 + cc

    partner = (row_of(o, i, 1 - core), c)
    zs_of = [flip(o, d, outer) for d in range(outer)]
    xs_of = [flip(i, d, inner) for d in range(inner)]
    y_far = [(c + d) % n_c for d in range(1, n_c)]
    y_src = [(c - d + n_c) % n_c for d in range(1, n_c)]

    def tile_copy(ch):
        at = pl.ds(ch * step, step)
        return pltpu.make_async_copy(tiles.at[0, 0, at], tbuf.at[at], tile_sem.at[ch])

    own = [
        pltpu.make_async_copy(src, dst, own_sem.at[q])
        for q, (src, dst) in enumerate(
            [
                (right, cv.at[pl.ds(r * piece, piece)]),
                (left, rv.at[pl.ds(c * piece, piece)]),
                (row_at, row_s),
                (col_at, col_s),
                (row_at, row_v),
                (col_at, col_v),
            ]
        )
    ]
    for copy in own:
        copy.start()

    barrier = pltpu.get_barrier_semaphore()
    near = [
        ((i + d) % inner, (core + e) % 2, (i - d + inner) % inner)
        for d in range(inner)
        for e in range(2)
        if d or e
    ]
    wide_set = [
        ((o + d) % outer, (c + e) % n_c, (o - d + outer) % outer, (c - e + n_c) % n_c)
        for d in range(outer)
        for e in range(n_c)
        if d or e
    ]
    near_peers = [(row_of(o, x, cc), c) for x, cc, _ in near]
    near_src = [x * 2 + cc for _, cc, x in near]
    wide_peers = [(row_of(z, i, core), y) for z, y, _, _ in wide_set]
    wide_src = [z * n_c + y for _, _, z, y in wide_set]
    peers = near_peers + wide_peers
    for peer in peers:
        pl.semaphore_signal(barrier, inc=1, device_id=peer, device_id_type=MESH)
    pl.semaphore_wait(barrier, len(peers))

    sent = []

    def send(src, dst, sem, peer):
        copy = pltpu.make_async_remote_copy(
            src_ref=src,
            dst_ref=dst,
            send_sem=send_sem.at[len(sent)],
            recv_sem=sem,
            device_id=peer,
            device_id_type=MESH,
        )
        copy.start()
        sent.append(copy)

    def landed(ref, sem):
        pltpu.make_async_remote_copy(
            src_ref=ref,
            dst_ref=ref,
            send_sem=send_sem.at[0],
            recv_sem=sem,
            device_id=partner,
            device_id_type=MESH,
        ).wait_recv()

    def cv_at(rr):
        return cv.at[pl.ds(rr * piece, piece)]

    def rv_at(cc):
        return rv.at[pl.ds(cc * piece, piece)]

    for y in y_far:
        send(left, rv_at(c), left_sem.at[c], (r, y))
    for x in xs_of[1:]:
        send(right, cv_at(r), right_sem.at[r], (row_of(o, x, core), c))
    for z in zs_of[1:]:
        send(right, cv_at(r), right_sem.at[r], (row_of(z, i, core), c))
    send(right, cv_at(r), right_sem.at[r], partner)
    for ch in range(chunks):
        tile_copy(ch).start()

    def take_z(d):
        with scope("take_z%d" % d):
            got = row_of(zs_of[d], i, core)
            landed(cv_at(got), right_sem.at[got])
            for x in xs_of[1:]:
                send(cv_at(got), cv_at(got), right_sem.at[got], (row_of(o, x, core), c))
            send(cv_at(got), cv_at(got), right_sem.at[got], partner)

    def take_x(d):
        with scope("take_x%d" % d):
            for x in xs_of[1:]:
                got = row_of(zs_of[d], x, core)
                landed(cv_at(got), right_sem.at[got])
                send(cv_at(got), cv_at(got), right_sem.at[got], partner)

    def take_core(d):
        with scope("take_c%d" % d):
            for x in xs_of:
                got = row_of(zs_of[d], x, 1 - core)
                landed(cv_at(got), right_sem.at[got])

    def images(ch, vec_ref, index, limit, turned):
        def body(g, carry):
            for u in range(0, GROUP, PAIR):
                s = ch * step + g * GROUP + u
                xs = [vec_ref[jnp.minimum(index[0, s + q], limit - 1)] for q in range(PAIR)]
                ts = [tbuf[s + q] for q in range(PAIR)]
                dims = across if turned else plain
                got = mul(jnp.concatenate(xs, 0), jnp.concatenate(ts, 0 if turned else 1), dims)
                for q in range(PAIR):
                    block = got[q * vecs : (q + 1) * vecs, q * side : (q + 1) * side]
                    prod[pl.ds((s + q) * wide, vecs), :] = block
            return carry

        lax.fori_loop(0, step // GROUP, body, 0)

    plain = (((1,), (0,)), ((), ()))
    across = (((1,), (1,)), ((), ()))

    def gather_sums(index_v, rows, target, first=0, last=vecs // KGROUP):
        pick = lax.broadcasted_iota(jnp.int32, (rows, slots), 0) == index_v[...]
        pick = jnp.where(pick, 1.0, 0.0).astype(BF16)
        pick = jnp.concatenate([pick, pick], 1)

        def body(g, carry):
            for u in range(0, KGROUP, PAIR):
                k = g * KGROUP + u
                terms = [split(prod[pl.ds(k + q, slots, stride=wide), :]) for q in range(PAIR)]
                high = jnp.concatenate([t[0] for t in terms], 1)
                low = jnp.concatenate([t[1] for t in terms], 1)
                got = mul(pick, jnp.concatenate([high, low], 0))
                for q in range(PAIR):
                    block = got[:, q * side : (q + 1) * side]
                    target[pl.ds(k + q, rows, stride=wide), :] = block
            return carry

        lax.fori_loop(first, last, body, 0)

    def encode(block_of, q_ref, s_ref):
        scales = []
        for t in range(piece):
            block = block_of(t)
            top = jnp.maximum(jnp.max(jnp.abs(block), axis=0, keepdims=True), LEAST)
            q_ref[t * vecs : (t + 1) * vecs] = (
                jnp.round(block * (TOP / top)).astype(jnp.int32).astype(jnp.int16)
            )
            scales.append(top * (1.0 / TOP))
        s_ref[...] = jnp.concatenate(scales, 0)

    def decode(q_ref, s_ref, t):
        code = q_ref[t * vecs : (t + 1) * vecs].astype(jnp.int32).astype(F32)
        return code * s_ref[t : t + 1]

    def pair_sum(dz, dx, t):
        at = row_of(zs_of[dz], xs_of[dx], core) * part + t * wide
        return zp[pl.ds(at, vecs), :] + zc[dz * inner + dx, t * wide : t * wide + vecs]

    powers = [1 << b for b in range(outer.bit_length() - 1)]
    z_order = [*range(outer - 1, 0, -2), *range(outer - 2, 0, -2), 0]

    def give_core():
        with scope("give_core"):
            for dx in range(inner - 1, -1, -1):
                for dz in z_order:
                    at = pl.ds(row_of(zs_of[dz], xs_of[dx], 1 - core) * part, part)
                    slot = dz * inner + dx
                    send(zp.at[at], zc.at[slot], zc_sem.at[slot], partner)

    def give_x(dz):
        with scope("give_x%d" % dz):
            for dx in range(inner - 1, 0, -1):
                slot = dz * inner + dx
                landed(zc.at[slot], zc_sem.at[slot])
                out = qx_out.at[dx - 1, dz], sx_out.at[dx - 1, dz]
                encode(functools.partial(pair_sum, dz, dx), *out)
                peer = (row_of(o, xs_of[dx], core), c)
                send(out[0], qx.at[dx - 1, dz], zx_sem.at[dx - 1, dz], peer)
                send(out[1], sx.at[dx - 1, dz], sx_sem.at[dx - 1, dz], peer)

    def own_x():
        with scope("own_x"):
            for dz in range(outer - 1, -1, -1):
                landed(zc.at[dz * inner], zc_sem.at[dz * inner])

    def low_bit(d):
        return d & -d

    def merged(dz):
        return [dz | b for b in powers if b < (low_bit(dz) or outer)]

    def plane_sum(dz, t):
        total = pair_sum(dz, 0, t)
        for d in range(1, inner):
            total = total + decode(qx.at[d - 1, dz], sx.at[d - 1, dz], t)
        return total

    def arrived(d):
        landed(qz.at[d - 1], zz_sem.at[d - 1])
        landed(sz.at[d - 1], sz_sem.at[d - 1])

    def give_z(dz):
        with scope("give_z%d" % dz):
            for d in range(1, inner):
                landed(qx.at[d - 1, dz], zx_sem.at[d - 1, dz])
                landed(sx.at[d - 1, dz], sx_sem.at[d - 1, dz])
            if dz == 0:
                for t in range(piece):
                    zs[t * vecs : (t + 1) * vecs] = plane_sum(0, t)
                return
            for d in merged(dz):
                arrived(d)

            def block(t):
                total = plane_sum(dz, t)
                for d in merged(dz):
                    total = total + decode(qz.at[d - 1], sz.at[d - 1], t)
                return total

            out = qz_out.at[dz - 1], sz_out.at[dz - 1]
            encode(block, *out)
            peer = (row_of(zs_of[low_bit(dz)], i, core), c)
            send(out[0], qz.at[dz - 1], zz_sem.at[dz - 1], peer)
            send(out[1], sz.at[dz - 1], sz_sem.at[dz - 1], peer)

    def gram_plane(d, total):
        with scope("gram%d" % d):
            sums, mates = [], []
            for dx in range(inner):
                p = row_of(zs_of[d], xs_of[dx], core)
                for t in range(piece):
                    high, low = split(pair_sum(d, dx, t))
                    sums.append(jnp.concatenate([high, low], 0))
                    mates.append(cv[p * piece + t])
            return total + mul(jnp.concatenate(sums, 1), jnp.concatenate(mates, 1), across)

    def spread(value, buf, base, me, far):
        with scope("spread%d" % base):
            buf[me] = value
            for peer in far:
                send(buf.at[me], buf.at[me], g_sem.at[base + me], peer)

    def collect(buf, base, src):
        with scope("collect%d" % base):
            for q in src:
                landed(buf.at[q], g_sem.at[base + q])
            total = buf[0]
            for q in range(1, buf.shape[0]):
                total = total + buf[q]
            return total

    with scope("wait_left"):
        for copy in own:
            copy.wait()
        for y in y_src:
            landed(rv_at(y), left_sem.at[y])

    def left_images(first, last):
        with scope("imgL%d" % first):
            for ch in range(first, last):
                tile_copy(ch).wait()
                images(ch, rv, row_s, block_rows, False)

    def right_images(first, last):
        with scope("imgR%d" % first):
            for ch in range(first, last):
                images(ch, cv, col_s, block_cols, True)

    def maybe(step, d):
        if d < outer:
            step(d)

    left_images(0, 2)
    maybe(take_z, 1)
    left_images(2, 5)
    take_x(0)
    left_images(5, chunks)
    maybe(take_z, 2)
    groups = vecs // KGROUP
    with scope("gatherZa"):
        gather_sums(col_v, block_cols, zp, 0, groups // 2)
    for d in range(3, outer):
        take_z(d)
    with scope("gatherZb"):
        gather_sums(col_v, block_cols, zp, groups // 2, groups)
    give_core()
    maybe(take_x, 1)
    maybe(take_x, 2)
    for d in z_order:
        give_x(d)
    for d in range(3, outer):
        take_x(d)
    own_x()
    total = jnp.zeros((2 * vecs, vecs), F32)
    for d in range(outer):
        total = gram_plane(d, total)
    spread(total[:vecs] + total[vecs:], gb, 2 * inner, o * n_c + c, wide_peers)
    for d in range(outer):
        take_core(d)

    todo = list(z_order)
    for ch in range(0, chunks, 2):
        right_images(ch, ch + 2)
        if todo and todo[0] & 1:
            give_z(todo.pop(0))
        if ch + 4 == chunks:
            spread(collect(gb, 2 * inner, wide_src), ga, 0, i * 2 + core, near_peers)
    for d in todo[:-1]:
        give_z(d)
    with scope("gatherY"):
        gather_sums(row_v, block_rows, yp)
    with scope("give_y"):
        for d, y in enumerate(y_far):
            encode(lambda t: yp[pl.ds(y * part + t * wide, vecs), :], qy_out.at[d], sy_out.at[d])
            send(qy_out.at[d], qy.at[d], zy_sem.at[d], (r, y))
            send(sy_out.at[d], sy.at[d], sy_sem.at[d], (r, y))
    give_z(0)
    gram = collect(ga, 0, near_src)
    with scope("correct"):
        gram = gram * (block_cols * n_c * side) ** (-0.5)
        out_g[...] = gram
        high, low = split(gram)
        turned_high, turned_low = split(gram.T)
        for t in range(piece):
            mine = cv[r * piece + t]
            out_y[t] = yp[pl.ds(c * part + t * wide, vecs), :] - (
                mul(turned_high, mine) + mul(turned_low, mine)
            )
            mine = rv[c * piece + t]
            out_z[t] = zs[t * vecs : (t + 1) * vecs] - (mul(high, mine) + mul(low, mine))
    with scope("wait_y"):
        for d in range(n_c - 1):
            landed(qy.at[d], zy_sem.at[d])
            landed(sy.at[d], sy_sem.at[d])
    with scope("out_y"):
        for t in range(piece):
            total = out_y[t]
            for d in range(n_c - 1):
                total = total + decode(qy.at[d], sy.at[d], t)
            out_y[t] = total
    with scope("wait_z"):
        for d in powers:
            arrived(d)
    with scope("out_z"):
        for t in range(piece):
            total = out_z[t]
            for d in powers:
                total = total + decode(qz.at[d - 1], sz.at[d - 1], t)
            out_z[t] = total
    with scope("wait_send"):
        for copy in sent:
            copy.wait_send()


def flush(*refs):
    sem = refs[-1]
    half = len(refs) // 2
    copies = [
        pltpu.make_async_copy(refs[q], refs[half + q], sem.at[q]) for q in range(half)
    ]
    for copy in copies:
        copy.start()
    for copy in copies:
        copy.wait()


def solution(mesh):
    n_r, n_c = mesh.shape["row"], mesh.shape["col"]
    half = n_r // 2
    inner = 1 << ((half.bit_length() - 1) // 2)
    outer = half // inner

    def per_device(tiles, tile_row, tile_col, right_vecs, left_vecs):
        slots, side = tiles.shape[2], tiles.shape[3]
        piece, vecs, _ = right_vecs.shape
        chunks = 8
        wide = vecs + PAD
        part = piece * wide
        block_rows, block_cols = piece * n_c, piece * n_r
        planes = outer * inner
        near, far, mates = max(inner - 1, 1), max(outer - 1, 1), max(n_c - 1, 1)
        sends = (
            3 * (n_c - 1)
            + (outer - 1)
            + (inner - 1)
            + 1
            + (outer - 1) * inner
            + outer * (inner - 1)
            + planes
            + 2 * outer * (inner - 1)
            + 2 * (outer - 1)
            + (2 * inner - 1)
            + (outer * n_c - 1)
        )
        vmem = pl.BlockSpec(memory_space=pltpu.VMEM)
        dma = pltpu.SemaphoreType.DMA
        shapes = [(piece, vecs, side), (piece, vecs, side), (vecs, vecs)]
        held = pl.pallas_call(
            functools.partial(kernel, (n_r, n_c, outer, inner, chunks)),
            out_shape=tuple(pltpu.VMEM(shape, F32) for shape in shapes),
            in_specs=[pl.BlockSpec(memory_space=pltpu.HBM)] * 5,
            out_specs=(vmem, vmem, vmem),
            scratch_shapes=[
                pltpu.VMEM((slots, side, side), BF16),
                pltpu.VMEM((block_cols, vecs, side), BF16),
                pltpu.VMEM((block_rows, vecs, side), BF16),
                pltpu.VMEM((slots * wide, side), F32),
                pltpu.VMEM((block_cols * wide, side), F32),
                pltpu.VMEM((planes, part, side), F32),
                pltpu.VMEM((piece * vecs, side), F32),
                *[
                    pltpu.VMEM(lead + shape, kind)
                    for lead in [(near, outer)] * 2 + [(far,)] * 2
                    for shape, kind in [((piece * vecs, side), jnp.int16), ((piece, side), F32)]
                ],
                pltpu.VMEM((block_rows * wide, side), F32),
                *[
                    pltpu.VMEM((mates,) + shape, kind)
                    for shape, kind in [((piece * vecs, side), jnp.int16), ((piece, side), F32)] * 2
                ],
                pltpu.VMEM((2 * inner, vecs, vecs), F32),
                pltpu.VMEM((outer * n_c, vecs, vecs), F32),
                *[pltpu.SMEM((1, slots), jnp.int32)] * 2,
                *[pltpu.VMEM((1, slots), jnp.int32)] * 2,
                dma((6,)),
                dma((chunks,)),
                dma((sends,)),
                dma((n_c,)),
                dma((n_r,)),
                dma((planes,)),
                *[dma((near, outer))] * 2,
                *[dma((far,))] * 2,
                *[dma((mates,))] * 2,
                dma((2 * inner + outer * n_c,)),
            ],
            compiler_params=pltpu.CompilerParams(
                collective_id=0, has_side_effects=True, vmem_limit_bytes=44 * 1024 * 1024
            ),
            name="arnoldi_step",
        )(
            *[
                pltpu.with_memory_space_constraint(x, pltpu.HBM)
                for x in (
                    tile_row.reshape(1, slots),
                    tile_col.reshape(1, slots),
                    right_vecs,
                    left_vecs,
                    tiles,
                )
            ]
        )
        held = [pltpu.with_memory_space_constraint(x, pltpu.VMEM) for x in held]
        return pl.pallas_call(
            flush,
            out_shape=tuple(jax.ShapeDtypeStruct(shape, F32) for shape in shapes),
            in_specs=[vmem] * len(shapes),
            out_specs=(pl.BlockSpec(memory_space=pl.ANY),) * len(shapes),
            scratch_shapes=[dma((len(shapes),))],
            name="flush",
        )(*held)

    placed = (
        P("row", "col", None, None, None),
        P("row", "col", None),
        P("row", "col", None),
        P(("row", "col"), None, None),
        P(("row", "col"), None, None),
    )
    return jax.shard_map(
        per_device,
        mesh=mesh,
        in_specs=placed,
        out_specs=(P(("row", "col"), None, None), P(("row", "col"), None, None), P()),
        check_vma=False,
    )
```

```python
import functools
from contextlib import nullcontext as scope

import jax
import jax.numpy as jnp
from jax import lax
from jax.experimental import pallas as pl
from jax.experimental.pallas import tpu as pltpu
from jax.sharding import PartitionSpec as P

MESH = pl.DeviceIdType.MESH
F32 = jnp.float32
BF16 = jnp.bfloat16
PAIR = 2
HALVES = 2
TILE_COPIES = 2
RIGHT, LEFT, PAIRED, ALONG_X, ALONG_Z, ALONG_Y, GRAM = range(7)
TOP = 32767.0
LEAST = 2.0**-110
PAD = 1


def split(value):
    high = value.astype(BF16)
    low = (value - high.astype(F32)).astype(BF16)
    return high, low


def mul(a, b, dims=(((1,), (0,)), ((), ()))):
    return lax.dot_general(a, b, dims, preferred_element_type=F32)


def flip(at, d, size):
    total, bit = 0, 1
    while bit < size:
        digit = at // bit % 2
        total = total + bit * (1 - digit if d & bit else digit)
        bit *= 2
    return total


def kernel(
    sizes,
    row_at,
    col_at,
    right,
    left,
    tiles,
    out_y,
    out_z,
    out_g,
    tbuf,
    cv,
    rv,
    prod,
    zp,
    zc,
    zs,
    qx_out,
    sx_out,
    qx,
    sx,
    qz_out,
    sz_out,
    qz,
    sz,
    yp,
    qy_out,
    sy_out,
    qy,
    sy,
    ga,
    gb,
    row_s,
    col_s,
    row_v,
    col_v,
    own_sem,
    tile_sem,
    send_sem,
    left_sem,
    right_sem,
    zc_sem,
    zx_sem,
    zz_sem,
    zy_sem,
    g_sem,
):
    n_r, n_c, outer, inner, chunks = sizes
    piece, vecs, side = right.shape
    slots = tbuf.shape[0]
    step = slots // chunks
    block_rows = piece * n_c
    block_cols = piece * n_r
    wide = vecs + PAD
    part = piece * wide
    r = lax.axis_index("row")
    c = lax.axis_index("col")
    core = r % 2
    i = (r // 2) % inner
    o = r // (2 * inner)

    def row_of(oo, ii, cc):
        return (oo * inner + ii) * 2 + cc

    partner = (row_of(o, i, 1 - core), c)
    zs_of = [flip(o, d, outer) for d in range(outer)]
    xs_of = [flip(i, d, inner) for d in range(inner)]
    y_far = [(c + d) % n_c for d in range(1, n_c)]
    y_src = [(c - d + n_c) % n_c for d in range(1, n_c)]

    def tile_copy(ch):
        at = pl.ds(ch * (slots // TILE_COPIES), slots // TILE_COPIES)
        return pltpu.make_async_copy(tiles.at[0, 0, at], tbuf.at[at], tile_sem.at[ch])

    own = [
        pltpu.make_async_copy(src, dst, own_sem.at[q])
        for q, (src, dst) in enumerate(
            [
                (right, cv.at[pl.ds(r * piece, piece)]),
                (left, rv.at[pl.ds(c * piece, piece)]),
                (row_at, row_s),
                (col_at, col_s),
                (row_at, row_v),
                (col_at, col_v),
            ]
        )
    ]
    for copy in own:
        copy.start()

    barrier = pltpu.get_barrier_semaphore()
    near = [
        ((i + d) % inner, (core + e) % 2)
        for d in range(inner)
        for e in range(2)
        if d or e
    ]
    wide_set = [
        ((o + d) % outer, (c + e) % n_c)
        for d in range(outer)
        for e in range(n_c)
        if d or e
    ]
    near_peers = [(row_of(o, x, cc), c) for x, cc in near]
    wide_peers = [(row_of(z, i, core), y) for z, y in wide_set]
    peers = near_peers + wide_peers
    for peer in peers:
        pl.semaphore_signal(barrier, inc=1, device_id=peer, device_id_type=MESH)
    pl.semaphore_wait(barrier, len(peers))

    def send(src, dst, sem, peer, group):
        pltpu.make_async_remote_copy(
            src_ref=src,
            dst_ref=dst,
            send_sem=send_sem.at[group],
            recv_sem=sem,
            device_id=peer,
            device_id_type=MESH,
        ).start()

    def left_here(ref, group):
        pltpu.make_async_remote_copy(
            src_ref=ref,
            dst_ref=ref,
            send_sem=send_sem.at[group],
            recv_sem=send_sem.at[group],
            device_id=partner,
            device_id_type=MESH,
        ).wait_send()

    def landed(ref, sem):
        pltpu.make_async_remote_copy(
            src_ref=ref,
            dst_ref=ref,
            send_sem=send_sem.at[0],
            recv_sem=sem,
            device_id=partner,
            device_id_type=MESH,
        ).wait_recv()

    def cv_at(rr):
        return cv.at[pl.ds(rr * piece, piece)]

    def rv_at(cc):
        return rv.at[pl.ds(cc * piece, piece)]

    for y in y_far:
        send(left, rv_at(c), left_sem.at[c], (r, y), LEFT)
    for x in xs_of[1:]:
        send(right, cv_at(r), right_sem.at[r], (row_of(o, x, core), c), RIGHT)
    for z in zs_of[1:]:
        send(right, cv_at(r), right_sem.at[r], (row_of(z, i, core), c), RIGHT)
    send(right, cv_at(r), right_sem.at[r], partner, RIGHT)
    for ch in range(TILE_COPIES):
        tile_copy(ch).start()

    def take_z(d):
        with scope("take_z%d" % d):
            got = row_of(zs_of[d], i, core)
            landed(cv_at(got), right_sem.at[got])
            for x in xs_of[1:]:
                send(cv_at(got), cv_at(got), right_sem.at[got], (row_of(o, x, core), c), RIGHT)
            send(cv_at(got), cv_at(got), right_sem.at[got], partner, RIGHT)

    def take_x(d):
        with scope("take_x%d" % d):
            for x in xs_of[1:]:
                got = row_of(zs_of[d], x, core)
                landed(cv_at(got), right_sem.at[got])
                send(cv_at(got), cv_at(got), right_sem.at[got], partner, RIGHT)

    def take_core(d):
        with scope("take_c%d" % d):
            for x in xs_of:
                got = row_of(zs_of[d], x, 1 - core)
                landed(cv_at(got), right_sem.at[got])

    def images(first, last, vec_ref, index, limit, turned):
        for s in range(first * step, last * step, PAIR):
            xs = [vec_ref[jnp.minimum(index[0, s + q], limit - 1)] for q in range(PAIR)]
            ts = [tbuf[s + q] for q in range(PAIR)]
            dims = across if turned else plain
            got = mul(jnp.concatenate(xs, 0), jnp.concatenate(ts, 0 if turned else 1), dims)
            for q in range(PAIR):
                block = got[q * vecs : (q + 1) * vecs, q * side : (q + 1) * side]
                prod[pl.ds((s + q) * wide, vecs), :] = block

    plain = (((1,), (0,)), ((), ()))
    across = (((1,), (1,)), ((), ()))

    def gather_sums(index_v, rows, target, first, last):
        pick = lax.broadcasted_iota(jnp.int32, (rows, slots), 0) == index_v[...]
        pick = jnp.where(pick, 1.0, 0.0).astype(BF16)
        pick = jnp.concatenate([pick, pick], 1)
        for k in range(first, last, PAIR):
            terms = [split(prod[pl.ds(k + q, slots, stride=wide), :]) for q in range(PAIR)]
            high = jnp.concatenate([t[0] for t in terms], 1)
            low = jnp.concatenate([t[1] for t in terms], 1)
            got = mul(pick, jnp.concatenate([high, low], 0))
            for q in range(PAIR):
                block = got[:, q * side : (q + 1) * side]
                target[pl.ds(k + q, rows, stride=wide), :] = block

    def encode(block_of, q_ref, s_ref, rows=vecs):
        scales = []
        for t in range(piece):
            block = block_of(t)
            top = jnp.maximum(jnp.max(jnp.abs(block), axis=0, keepdims=True), LEAST)
            q_ref[t * rows : (t + 1) * rows] = (
                jnp.round(block * (TOP / top)).astype(jnp.int32).astype(jnp.int16)
            )
            scales.append(top * (1.0 / TOP))
        s_ref[...] = jnp.concatenate(scales, 0)

    def decode(q_ref, s_ref, t, rows=vecs):
        code = q_ref[t * rows : (t + 1) * rows].astype(jnp.int32).astype(F32)
        return code * s_ref[t : t + 1]

    def post(out, dst, sem, peer, group, rows=vecs):
        codes = pl.ds(0, piece * rows)
        send(out[0].at[codes], dst[0].at[codes], sem, peer, group)
        send(out[1], dst[1], sem, peer, group)

    def pair_sum(dz, dx, t):
        at = row_of(zs_of[dz], xs_of[dx], core) * part + t * wide
        return zp[pl.ds(at, vecs), :] + zc[dx * outer + dz, t * wide : t * wide + vecs]

    merging, middle = outer == 4, (o + 1) // 2 % 2
    z_order = list(range(outer - 1, -1, -1))

    def give_core():
        with scope("give_core"):
            for dx in range(inner - 1, -1, -1):
                for dz in z_order:
                    at = pl.ds(row_of(zs_of[dz], xs_of[dx], 1 - core) * part, part)
                    slot = dx * outer + dz
                    sem = zc_sem.at[slot - outer + 1 if dx else 0]
                    send(zp.at[at], zc.at[slot], sem, partner, PAIRED)

    def paired(dz):
        for dx in range(1, inner):
            slot = dx * outer + dz
            landed(zc.at[slot], zc_sem.at[slot - outer + 1])

    def give_x(dz):
        with scope("give_x%d" % dz):
            for dx in range(inner - 1, 0, -1):
                out = qx_out.at[dx - 1, dz], sx_out.at[dx - 1, dz]
                encode(functools.partial(pair_sum, dz, dx), *out)
                peer = (row_of(o, xs_of[dx], core), c)
                dst = qx.at[dx - 1, dz], sx.at[dx - 1, dz]
                post(out, dst, zx_sem.at[dx - 1, dz], peer, ALONG_X)

    def own_x():
        with scope("own_x"):
            landed(zc.at[pl.ds(0, outer)], zc_sem.at[0])

    def plane_sum(dz, t):
        total = pair_sum(dz, 0, t)
        for d in range(1, inner):
            total = total + decode(qx.at[d - 1, dz], sx.at[d - 1, dz], t)
        return total

    def arrived(d):
        landed(qz.at[d], zz_sem.at[d])

    def encode_z(dz, extra):
        def block(t):
            total = plane_sum(dz, t)
            for d in extra:
                total = total + decode(qz.at[d], sz.at[d], t)
            return total

        encode(block, qz_out.at[dz - 1], sz_out.at[dz - 1])

    def give_z(dz, extra=()):
        with scope("give_z%d" % dz):
            for d in range(1, inner):
                landed(qx.at[d - 1, dz], zx_sem.at[d - 1, dz])
            if dz == 0:
                for t in range(piece):
                    zs[t * vecs : (t + 1) * vecs] = plane_sum(0, t)
                return
            at, z = dz - 1, zs_of[dz]
            if merging and dz == 3:
                at, z = 3 - middle, zs_of[1] + middle * (zs_of[3] - zs_of[1])
            if extra:
                arrived(extra[0])
            encode_z(dz, extra)
            out = qz_out.at[dz - 1], sz_out.at[dz - 1]
            post(out, (qz.at[at], sz.at[at]), zz_sem.at[at], (row_of(z, i, core), c), ALONG_Z)

    def gram_plane(d, total):
        with scope("gram%d" % d):
            sums, mates = [], []
            for dx in range(inner):
                p = row_of(zs_of[d], xs_of[dx], core)
                for t in range(piece):
                    high, low = split(pair_sum(d, dx, t))
                    sums.append(jnp.concatenate([high, low], 0))
                    mates.append(cv[p * piece + t])
            return total + mul(jnp.concatenate(sums, 1), jnp.concatenate(mates, 1), across)

    def spread(value, buf, stage, me, far):
        with scope("spread%d" % stage):
            buf[me] = value
            for peer in far:
                send(buf.at[me], buf.at[me], g_sem.at[stage], peer, GRAM + stage)

    def collect(buf, stage):
        with scope("collect%d" % stage):
            landed(buf.at[pl.ds(0, buf.shape[0] - 1)], g_sem.at[stage])
            total = buf[0]
            for q in range(1, buf.shape[0]):
                total = total + buf[q]
            return total

    with scope("wait_left"):
        for copy in own:
            copy.wait()
        for y in y_src:
            landed(rv_at(y), left_sem.at[y])

    def left_images(first, last):
        with scope("imgL%d" % first):
            images(first, last, rv, row_s, block_rows, False)

    def right_images(first, last):
        with scope("imgR%d" % first):
            images(first, last, cv, col_s, block_cols, True)

    def maybe(step, d):
        if d < outer:
            step(d)

    maybe(take_z, 1)
    tile_copy(0).wait()
    left_images(0, chunks // 2)
    take_x(0)
    tile_copy(1).wait()
    left_images(chunks // 2, chunks)
    maybe(take_z, 2)
    with scope("gatherZ"):
        gather_sums(col_v, block_cols, zp, 0, vecs)
    for d in range(3, outer):
        take_z(d)
    give_core()
    maybe(take_x, 1)
    todo_x, todo_z = list(z_order), list(z_order)
    paired(todo_x[0])
    give_x(todo_x.pop(0))
    for d in range(2, outer):
        take_x(d)
    for d in todo_x:
        paired(d)
    while len(todo_x) > 2:
        give_x(todo_x.pop(0))
    own_x()
    total = jnp.zeros((2 * vecs, vecs), F32)
    for d in range(outer):
        total = gram_plane(d, total)
    spread(total[:vecs] + total[vecs:], gb, 1, o * n_c + c, wide_peers)
    while len(todo_x) > 1:
        give_x(todo_x.pop(0))
    for d in range(outer):
        take_core(d)
    first = todo_z.pop(0)
    pl.when(core == 0)(lambda: give_z(first))
    right_images(0, 2)
    give_x(todo_x.pop(0))
    pl.when(core == 1)(lambda: give_z(first))
    right_images(2, 5)
    if merging:
        pl.when(middle == 0)(lambda: give_z(2))
        todo_z.remove(2)
    right_images(5, chunks)
    while len(todo_z) > 1:
        give_z(todo_z.pop(0))

    def give_y(h):
        rows = vecs // HALVES
        with scope("gatherY%d" % h):
            gather_sums(row_v, block_rows, yp, h * rows, (h + 1) * rows)
        with scope("give_y%d" % h):
            for d, y in enumerate(y_far):
                out = qy_out.at[d, h], sy_out.at[d, h]
                start = y * part + h * rows
                encode(lambda t: yp[pl.ds(start + t * wide, rows), :], *out, rows)
                dst = qy.at[d, h], sy.at[d, h]
                post(out, dst, zy_sem.at[d, h], (r, y), ALONG_Y, rows)

    for h in range(HALVES):
        give_y(h)
    spread(collect(gb, 1), ga, 0, i * 2 + core, near_peers)
    if merging:
        pl.when(middle == 1)(lambda: give_z(2, [3]))
    give_z(0)
    gram = collect(ga, 0)
    with scope("correct"):
        gram = gram * (block_cols * n_c * side) ** (-0.5)
        out_g[...] = gram
        high, low = split(gram)
        turned_high, turned_low = split(gram.T)
        for t in range(piece):
            mine = cv[r * piece + t]
            out_y[t] = yp[pl.ds(c * part + t * wide, vecs), :] - (
                mul(turned_high, mine) + mul(turned_low, mine)
            )
            mine = rv[c * piece + t]
            out_z[t] = zs[t * vecs : (t + 1) * vecs] - (mul(high, mine) + mul(low, mine))
    for h in range(HALVES):
        rows = vecs // HALVES
        with scope("wait_y%d" % h):
            for d in range(n_c - 1):
                landed(qy.at[d, h], zy_sem.at[d, h])
        for t in range(piece):
            total = out_y[t, h * rows : (h + 1) * rows]
            for d in range(n_c - 1):
                total = total + decode(qy.at[d, h], sy.at[d, h], t, rows)
            out_y[t, h * rows : (h + 1) * rows] = total
    def add_z(slots_in):
        with scope("wait_z"):
            for d in slots_in:
                arrived(d)
        for t in range(piece):
            total = out_z[t]
            for d in slots_in:
                total = total + decode(qz.at[d], sz.at[d], t)
            out_z[t] = total

    if merging:
        pl.when(middle == 1)(lambda: add_z([0, 2, 1]))
        pl.when(middle == 0)(lambda: add_z([0, 1]))
    else:
        add_z(list(range(outer - 1)))
    with scope("wait_send"):
        left_here(cv.at[pl.ds(0, (n_r - 1) * piece)], RIGHT)
        left_here(rv.at[pl.ds(0, (n_c - 1) * piece)], LEFT)
        left_here(zc, PAIRED)
        left_here(qx_out, ALONG_X)
        left_here(qz_out, ALONG_Z)
        left_here(qy_out, ALONG_Y)
        left_here(ga.at[pl.ds(0, 2 * inner - 1)], GRAM)
        left_here(gb.at[pl.ds(0, outer * n_c - 1)], GRAM + 1)


def flush(*refs):
    sem = refs[-1]
    half = len(refs) // 2
    copies = [
        pltpu.make_async_copy(refs[q], refs[half + q], sem.at[q]) for q in range(half)
    ]
    for copy in copies:
        copy.start()
    for copy in copies:
        copy.wait()


def solution(mesh):
    n_r, n_c = mesh.shape["row"], mesh.shape["col"]
    half = n_r // 2
    inner = 1 << ((half.bit_length() - 1) // 2)
    outer = half // inner

    def per_device(tiles, tile_row, tile_col, right_vecs, left_vecs):
        slots, side = tiles.shape[2], tiles.shape[3]
        piece, vecs, _ = right_vecs.shape
        chunks = 8
        wide = vecs + PAD
        part = piece * wide
        block_rows, block_cols = piece * n_c, piece * n_r
        planes = outer * inner
        near, far, mates = max(inner - 1, 1), max(outer - 1, 1), max(n_c - 1, 1)
        rows = vecs // HALVES
        coded = [((piece * (vecs + 2), side), jnp.int16), ((piece, side), F32)]
        halved = [((piece * (rows + 2), side), jnp.int16), ((piece, side), F32)]
        vmem = pl.BlockSpec(memory_space=pltpu.VMEM)
        dma = pltpu.SemaphoreType.DMA
        shapes = [(piece, vecs, side), (piece, vecs, side), (vecs, vecs)]
        held = pl.pallas_call(
            functools.partial(kernel, (n_r, n_c, outer, inner, chunks)),
            out_shape=tuple(pltpu.VMEM(shape, F32) for shape in shapes),
            in_specs=[pl.BlockSpec(memory_space=pltpu.HBM)] * 5,
            out_specs=(vmem, vmem, vmem),
            scratch_shapes=[
                pltpu.VMEM((slots, side, side), BF16),
                pltpu.VMEM((block_cols, vecs, side), BF16),
                pltpu.VMEM((block_rows, vecs, side), BF16),
                pltpu.VMEM((slots * wide, side), F32),
                pltpu.VMEM((block_cols * wide, side), F32),
                pltpu.VMEM((planes, part, side), F32),
                pltpu.VMEM((piece * vecs, side), F32),
                *[
                    pltpu.VMEM(lead + shape, kind)
                    for lead in [(near, outer)] * 2 + [(far,), (outer,)]
                    for shape, kind in coded
                ],
                pltpu.VMEM((block_rows * wide, side), F32),
                *[pltpu.VMEM((mates, HALVES) + shape, kind) for shape, kind in halved * 2],
                pltpu.VMEM((2 * inner, vecs, vecs), F32),
                pltpu.VMEM((outer * n_c, vecs, vecs), F32),
                *[pltpu.SMEM((1, slots), jnp.int32)] * 2,
                *[pltpu.VMEM((1, slots), jnp.int32)] * 2,
                dma((6,)),
                dma((TILE_COPIES,)),
                dma((GRAM + 2,)),
                dma((n_c,)),
                dma((n_r,)),
                dma((1 + (inner - 1) * outer,)),
                dma((near, outer)),
                dma((outer,)),
                dma((mates, HALVES)),
                dma((2,)),
            ],
            compiler_params=pltpu.CompilerParams(
                collective_id=0, has_side_effects=True, vmem_limit_bytes=44 * 1024 * 1024
            ),
            name="arnoldi_step",
        )(
            *[
                pltpu.with_memory_space_constraint(x, pltpu.HBM)
                for x in (
                    tile_row.reshape(1, slots),
                    tile_col.reshape(1, slots),
                    right_vecs,
                    left_vecs,
                    tiles,
                )
            ]
        )
        held = [pltpu.with_memory_space_constraint(x, pltpu.VMEM) for x in held]
        return pl.pallas_call(
            flush,
            out_shape=tuple(jax.ShapeDtypeStruct(shape, F32) for shape in shapes),
            in_specs=[vmem] * len(shapes),
            out_specs=(pl.BlockSpec(memory_space=pl.ANY),) * len(shapes),
            scratch_shapes=[dma((len(shapes),))],
            name="flush",
        )(*held)

    placed = (
        P("row", "col", None, None, None),
        P("row", "col", None),
        P("row", "col", None),
        P(("row", "col"), None, None),
        P(("row", "col"), None, None),
    )
    return jax.shard_map(
        per_device,
        mesh=mesh,
        in_specs=placed,
        out_specs=(P(("row", "col"), None, None), P(("row", "col"), None, None), P()),
        check_vma=False,
    )
```

```python
import functools
from contextlib import nullcontext as scope

import jax
import jax.numpy as jnp
from jax import lax
from jax.experimental import pallas as pl
from jax.experimental.pallas import tpu as pltpu
from jax.sharding import PartitionSpec as P

MESH = pl.DeviceIdType.MESH
F32 = jnp.float32
BF16 = jnp.bfloat16
PAIR = 2
HALVES = 2
TILE_COPIES = 2
RIGHT, LEFT, PAIRED, ALONG_X, ALONG_Z, ALONG_Y, GRAM = range(7)
TOP = 32767.0
LEAST = 2.0**-110
PAD = 1


def split(value):
    high = value.astype(BF16)
    low = (value - high.astype(F32)).astype(BF16)
    return high, low


def mul(a, b, dims=(((1,), (0,)), ((), ()))):
    return lax.dot_general(a, b, dims, preferred_element_type=F32)


def flip(at, d, size):
    total, bit = 0, 1
    while bit < size:
        digit = at // bit % 2
        total = total + bit * (1 - digit if d & bit else digit)
        bit *= 2
    return total


def kernel(
    sizes,
    row_at,
    col_at,
    right,
    left,
    tiles,
    out_y,
    out_z,
    out_g,
    tbuf,
    cv,
    rv,
    prod,
    zp,
    zc,
    zs,
    qx_out,
    sx_out,
    qx,
    sx,
    qz_out,
    sz_out,
    qz,
    sz,
    yp,
    qy_out,
    sy_out,
    qy,
    sy,
    ga,
    gb,
    row_s,
    col_s,
    row_v,
    col_v,
    own_sem,
    tile_sem,
    send_sem,
    left_sem,
    right_sem,
    core_sem,
    zc_sem,
    zx_sem,
    zz_sem,
    zy_sem,
    g_sem,
):
    n_r, n_c, outer, inner, chunks = sizes
    piece, vecs, side = right.shape
    slots = tbuf.shape[0]
    step = slots // chunks
    block_rows = piece * n_c
    block_cols = piece * n_r
    wide = vecs + PAD
    part = piece * wide
    r = lax.axis_index("row")
    c = lax.axis_index("col")
    core = r % 2
    i = (r // 2) % inner
    o = r // (2 * inner)

    def row_of(oo, ii, cc):
        return (oo * inner + ii) * 2 + cc

    partner = (row_of(o, i, 1 - core), c)
    zs_of = [flip(o, d, outer) for d in range(outer)]
    xs_of = [flip(i, d, inner) for d in range(inner)]
    y_far = [(c + d) % n_c for d in range(1, n_c)]
    y_src = [(c - d + n_c) % n_c for d in range(1, n_c)]

    def tile_copy(ch):
        at = pl.ds(ch * (slots // TILE_COPIES), slots // TILE_COPIES)
        return pltpu.make_async_copy(tiles.at[0, 0, at], tbuf.at[at], tile_sem.at[ch])

    own = [
        pltpu.make_async_copy(src, dst, own_sem.at[q])
        for q, (src, dst) in enumerate(
            [
                (right, cv.at[pl.ds(r * piece, piece)]),
                (left, rv.at[pl.ds(c * piece, piece)]),
                (row_at, row_s),
                (col_at, col_s),
                (row_at, row_v),
                (col_at, col_v),
            ]
        )
    ]
    for copy in own:
        copy.start()

    barrier = pltpu.get_barrier_semaphore()
    near = [
        ((i + d) % inner, (core + e) % 2)
        for d in range(inner)
        for e in range(2)
        if d or e
    ]
    wide_set = [
        ((o + d) % outer, (c + e) % n_c)
        for d in range(outer)
        for e in range(n_c)
        if d or e
    ]
    near_peers = [(row_of(o, x, cc), c) for x, cc in near]
    wide_peers = [(row_of(z, i, core), y) for z, y in wide_set]
    peers = near_peers + wide_peers
    for peer in peers:
        pl.semaphore_signal(barrier, inc=1, device_id=peer, device_id_type=MESH)
    pl.semaphore_wait(barrier, len(peers))

    def send(src, dst, sem, peer, group):
        pltpu.make_async_remote_copy(
            src_ref=src,
            dst_ref=dst,
            send_sem=send_sem.at[group],
            recv_sem=sem,
            device_id=peer,
            device_id_type=MESH,
        ).start()

    def left_here(ref, group):
        pltpu.make_async_remote_copy(
            src_ref=ref,
            dst_ref=ref,
            send_sem=send_sem.at[group],
            recv_sem=send_sem.at[group],
            device_id=partner,
            device_id_type=MESH,
        ).wait_send()

    def landed(ref, sem):
        pltpu.make_async_remote_copy(
            src_ref=ref,
            dst_ref=ref,
            send_sem=send_sem.at[0],
            recv_sem=sem,
            device_id=partner,
            device_id_type=MESH,
        ).wait_recv()

    def cv_at(rr):
        return cv.at[pl.ds(rr * piece, piece)]

    def rv_at(cc):
        return rv.at[pl.ds(cc * piece, piece)]

    for y in y_far:
        send(left, rv_at(c), left_sem.at[c], (r, y), LEFT)
    for x in xs_of[1:]:
        send(right, cv_at(r), right_sem.at[r // 2], (row_of(o, x, core), c), RIGHT)
    for z in zs_of[1:]:
        send(right, cv_at(r), right_sem.at[r // 2], (row_of(z, i, core), c), RIGHT)
    send(right, cv_at(r), core_sem.at[0], partner, RIGHT)
    for ch in range(TILE_COPIES):
        tile_copy(ch).start()

    def take_z(d):
        with scope("take_z%d" % d):
            got = row_of(zs_of[d], i, core)
            landed(cv_at(got), right_sem.at[got // 2])
            for x in xs_of[1:]:
                send(cv_at(got), cv_at(got), right_sem.at[got // 2], (row_of(o, x, core), c), RIGHT)
            send(cv_at(got), cv_at(got), core_sem.at[0], partner, RIGHT)

    def take_x(d):
        with scope("take_x%d" % d):
            for x in xs_of[1:]:
                got = row_of(zs_of[d], x, core)
                landed(cv_at(got), right_sem.at[got // 2])
                send(cv_at(got), cv_at(got), core_sem.at[0], partner, RIGHT)

    def take_core():
        with scope("take_core"):
            landed(cv.at[pl.ds(0, outer * inner * piece)], core_sem.at[0])

    def images(first, last, vec_ref, index, limit, turned):
        for s in range(first * step, last * step, PAIR):
            xs = [vec_ref[jnp.minimum(index[0, s + q], limit - 1)] for q in range(PAIR)]
            ts = [tbuf[s + q] for q in range(PAIR)]
            dims = across if turned else plain
            got = mul(jnp.concatenate(xs, 0), jnp.concatenate(ts, 0 if turned else 1), dims)
            for q in range(PAIR):
                block = got[q * vecs : (q + 1) * vecs, q * side : (q + 1) * side]
                prod[pl.ds((s + q) * wide, vecs), :] = block

    plain = (((1,), (0,)), ((), ()))
    across = (((1,), (1,)), ((), ()))

    def gather_sums(index_v, rows, target, first, last):
        pick = lax.broadcasted_iota(jnp.int32, (rows, slots), 0) == index_v[...]
        pick = jnp.where(pick, 1.0, 0.0).astype(BF16)
        pick = jnp.concatenate([pick, pick], 1)
        for k in range(first, last, PAIR):
            terms = [split(prod[pl.ds(k + q, slots, stride=wide), :]) for q in range(PAIR)]
            high = jnp.concatenate([t[0] for t in terms], 1)
            low = jnp.concatenate([t[1] for t in terms], 1)
            got = mul(pick, jnp.concatenate([high, low], 0))
            for q in range(PAIR):
                block = got[:, q * side : (q + 1) * side]
                target[pl.ds(k + q, rows, stride=wide), :] = block

    def encode(block_of, q_ref, s_ref, rows=vecs):
        scales = []
        for t in range(piece):
            block = block_of(t)
            top = jnp.maximum(jnp.max(jnp.abs(block), axis=0, keepdims=True), LEAST)
            q_ref[t * rows : (t + 1) * rows] = (
                jnp.round(block * (TOP / top)).astype(jnp.int32).astype(jnp.int16)
            )
            scales.append(top * (1.0 / TOP))
        s_ref[...] = jnp.concatenate(scales, 0)

    def decode(q_ref, s_ref, t, rows=vecs):
        code = q_ref[t * rows : (t + 1) * rows].astype(jnp.int32).astype(F32)
        return code * s_ref[t : t + 1]

    def post(out, dst, sem, peer, group, rows=vecs):
        codes = pl.ds(0, piece * rows)
        send(out[0].at[codes], dst[0].at[codes], sem, peer, group)
        send(out[1], dst[1], sem, peer, group)

    def pair_sum(dz, dx, t):
        at = row_of(zs_of[dz], xs_of[dx], core) * part + t * wide
        return zp[pl.ds(at, vecs), :] + zc[dx * outer + dz, t * wide : t * wide + vecs]

    merging, middle = outer == 4, (o + 1) // 2 % 2
    z_order = list(range(outer - 1, -1, -1))

    def give_core():
        with scope("give_core"):
            for dx in range(inner - 1, -1, -1):
                for dz in z_order:
                    at = pl.ds(row_of(zs_of[dz], xs_of[dx], 1 - core) * part, part)
                    slot = dx * outer + dz
                    sem = zc_sem.at[slot - outer + 1 if dx else 0]
                    send(zp.at[at], zc.at[slot], sem, partner, PAIRED)

    def paired(dz):
        for dx in range(1, inner):
            slot = dx * outer + dz
            landed(zc.at[slot], zc_sem.at[slot - outer + 1])

    def give_x(dz):
        with scope("give_x%d" % dz):
            for dx in range(inner - 1, 0, -1):
                out = qx_out.at[dx - 1, dz], sx_out.at[dx - 1, dz]
                encode(functools.partial(pair_sum, dz, dx), *out)
                peer = (row_of(o, xs_of[dx], core), c)
                dst = qx.at[dx - 1, dz], sx.at[dx - 1, dz]
                post(out, dst, zx_sem.at[dx - 1, dz], peer, ALONG_X)

    def own_x():
        with scope("own_x"):
            landed(zc.at[pl.ds(0, outer)], zc_sem.at[0])

    def plane_sum(dz, t):
        total = pair_sum(dz, 0, t)
        for d in range(1, inner):
            total = total + decode(qx.at[d - 1, dz], sx.at[d - 1, dz], t)
        return total

    def arrived(d):
        landed(qz.at[d], zz_sem.at[d])

    def encode_z(dz, extra):
        def block(t):
            total = plane_sum(dz, t)
            for d in extra:
                total = total + decode(qz.at[d], sz.at[d], t)
            return total

        encode(block, qz_out.at[dz - 1], sz_out.at[dz - 1])

    def give_z(dz, extra=()):
        with scope("give_z%d" % dz):
            for d in range(1, inner):
                landed(qx.at[d - 1, dz], zx_sem.at[d - 1, dz])
            if dz == 0:
                for t in range(piece):
                    zs[t * vecs : (t + 1) * vecs] = plane_sum(0, t)
                return
            at, z = dz - 1, zs_of[dz]
            if merging and dz == 3:
                at, z = 3 - middle, zs_of[1] + middle * (zs_of[3] - zs_of[1])
            if extra:
                arrived(extra[0])
            encode_z(dz, extra)
            out = qz_out.at[dz - 1], sz_out.at[dz - 1]
            post(out, (qz.at[at], sz.at[at]), zz_sem.at[at], (row_of(z, i, core), c), ALONG_Z)

    def gram_plane(d, total):
        with scope("gram%d" % d):
            sums, mates = [], []
            for dx in range(inner):
                p = row_of(zs_of[d], xs_of[dx], core)
                for t in range(piece):
                    high, low = split(pair_sum(d, dx, t))
                    sums.append(jnp.concatenate([high, low], 0))
                    mates.append(cv[p * piece + t])
            return total + mul(jnp.concatenate(sums, 1), jnp.concatenate(mates, 1), across)

    def spread(value, buf, stage, me, far):
        with scope("spread%d" % stage):
            buf[me] = value
            for peer in far:
                send(buf.at[me], buf.at[me], g_sem.at[stage], peer, GRAM + stage)

    def collect(buf, stage):
        with scope("collect%d" % stage):
            landed(buf.at[pl.ds(0, buf.shape[0] - 1)], g_sem.at[stage])
            total = buf[0]
            for q in range(1, buf.shape[0]):
                total = total + buf[q]
            return total

    with scope("wait_left"):
        for copy in own:
            copy.wait()
        for y in y_src:
            landed(rv_at(y), left_sem.at[y])

    def left_images(first, last):
        with scope("imgL%d" % first):
            images(first, last, rv, row_s, block_rows, False)

    def right_images(first, last):
        with scope("imgR%d" % first):
            images(first, last, cv, col_s, block_cols, True)

    def maybe(step, d):
        if d < outer:
            step(d)

    maybe(take_z, 1)
    tile_copy(0).wait()
    left_images(0, chunks // 2)
    take_x(0)
    tile_copy(1).wait()
    left_images(chunks // 2, chunks)
    maybe(take_z, 2)
    with scope("gatherZ"):
        gather_sums(col_v, block_cols, zp, 0, vecs)
    for d in range(3, outer):
        take_z(d)
    give_core()
    maybe(take_x, 1)
    todo_x, todo_z = list(z_order), list(z_order)
    paired(todo_x[0])
    give_x(todo_x.pop(0))
    for d in range(2, outer - 1):
        take_x(d)
    for d in todo_x:
        paired(d)
    while len(todo_x) > 2:
        give_x(todo_x.pop(0))
    own_x()
    total = jnp.zeros((2 * vecs, vecs), F32)
    for d in range(outer):
        if d == outer - 1 > 1:
            take_x(d)
        total = gram_plane(d, total)
    spread(total[:vecs] + total[vecs:], gb, 1, o * n_c + c, wide_peers)
    while len(todo_x) > 1:
        give_x(todo_x.pop(0))
    take_core()
    first = todo_z.pop(0)
    right_images(0, 2)
    give_z(first)
    give_x(todo_x.pop(0))
    right_images(2, 5)
    if merging:
        pl.when(middle == 0)(lambda: give_z(2))
        todo_z.remove(2)
    right_images(5, chunks)
    while len(todo_z) > 1:
        give_z(todo_z.pop(0))

    def give_y(h):
        rows = vecs // HALVES
        with scope("gatherY%d" % h):
            gather_sums(row_v, block_rows, yp, h * rows, (h + 1) * rows)
        with scope("give_y%d" % h):
            for d, y in enumerate(y_far):
                out = qy_out.at[d, h], sy_out.at[d, h]
                start = y * part + h * rows
                encode(lambda t: yp[pl.ds(start + t * wide, rows), :], *out, rows)
                dst = qy.at[d, h], sy.at[d, h]
                post(out, dst, zy_sem.at[d, h], (r, y), ALONG_Y, rows)

    for h in range(HALVES):
        give_y(h)
    spread(collect(gb, 1), ga, 0, i * 2 + core, near_peers)
    if merging:
        pl.when(middle == 1)(lambda: give_z(2, [3]))
    give_z(0)
    gram = collect(ga, 0)
    with scope("correct"):
        gram = gram * (block_cols * n_c * side) ** (-0.5)
        out_g[...] = gram
        high, low = split(gram)
        turned_high, turned_low = split(gram.T)
        for t in range(piece):
            mine = cv[r * piece + t]
            out_y[t] = yp[pl.ds(c * part + t * wide, vecs), :] - (
                mul(turned_high, mine) + mul(turned_low, mine)
            )
            mine = rv[c * piece + t]
            out_z[t] = zs[t * vecs : (t + 1) * vecs] - (mul(high, mine) + mul(low, mine))
    for h in range(HALVES):
        rows = vecs // HALVES
        with scope("wait_y%d" % h):
            for d in range(n_c - 1):
                landed(qy.at[d, h], zy_sem.at[d, h])
        for t in range(piece):
            total = out_y[t, h * rows : (h + 1) * rows]
            for d in range(n_c - 1):
                total = total + decode(qy.at[d, h], sy.at[d, h], t, rows)
            out_y[t, h * rows : (h + 1) * rows] = total
    def add_z(slots_in):
        with scope("wait_z"):
            for d in slots_in:
                arrived(d)
        for t in range(piece):
            total = out_z[t]
            for d in slots_in:
                total = total + decode(qz.at[d], sz.at[d], t)
            out_z[t] = total

    if merging:
        pl.when(middle == 1)(lambda: add_z([0, 2, 1]))
        pl.when(middle == 0)(lambda: add_z([0, 1]))
    else:
        add_z(list(range(outer - 1)))
    with scope("wait_send"):
        left_here(cv.at[pl.ds(0, (n_r - 1) * piece)], RIGHT)
        left_here(rv.at[pl.ds(0, (n_c - 1) * piece)], LEFT)
        left_here(zc, PAIRED)
        left_here(qx_out, ALONG_X)
        left_here(qz_out, ALONG_Z)
        left_here(qy_out, ALONG_Y)
        left_here(ga.at[pl.ds(0, 2 * inner - 1)], GRAM)
        left_here(gb.at[pl.ds(0, outer * n_c - 1)], GRAM + 1)


def flush(*refs):
    sem = refs[-1]
    half = len(refs) // 2
    copies = [
        pltpu.make_async_copy(refs[q], refs[half + q], sem.at[q]) for q in range(half)
    ]
    for copy in copies:
        copy.start()
    for copy in copies:
        copy.wait()


def solution(mesh):
    n_r, n_c = mesh.shape["row"], mesh.shape["col"]
    half = n_r // 2
    inner = 1 << ((half.bit_length() - 1) // 2)
    outer = half // inner

    def per_device(tiles, tile_row, tile_col, right_vecs, left_vecs):
        slots, side = tiles.shape[2], tiles.shape[3]
        piece, vecs, _ = right_vecs.shape
        chunks = 8
        wide = vecs + PAD
        part = piece * wide
        block_rows, block_cols = piece * n_c, piece * n_r
        planes = outer * inner
        near, far, mates = max(inner - 1, 1), max(outer - 1, 1), max(n_c - 1, 1)
        rows = vecs // HALVES
        coded = [((piece * (vecs + 2), side), jnp.int16), ((piece, side), F32)]
        halved = [((piece * (rows + 2), side), jnp.int16), ((piece, side), F32)]
        vmem = pl.BlockSpec(memory_space=pltpu.VMEM)
        dma = pltpu.SemaphoreType.DMA
        shapes = [(piece, vecs, side), (piece, vecs, side), (vecs, vecs)]
        held = pl.pallas_call(
            functools.partial(kernel, (n_r, n_c, outer, inner, chunks)),
            out_shape=tuple(pltpu.VMEM(shape, F32) for shape in shapes),
            in_specs=[pl.BlockSpec(memory_space=pltpu.HBM)] * 5,
            out_specs=(vmem, vmem, vmem),
            scratch_shapes=[
                pltpu.VMEM((slots, side, side), BF16),
                pltpu.VMEM((block_cols, vecs, side), BF16),
                pltpu.VMEM((block_rows, vecs, side), BF16),
                pltpu.VMEM((slots * wide, side), F32),
                pltpu.VMEM((block_cols * wide, side), F32),
                pltpu.VMEM((planes, part, side), F32),
                pltpu.VMEM((piece * vecs, side), F32),
                *[
                    pltpu.VMEM(lead + shape, kind)
                    for lead in [(near, outer)] * 2 + [(far,), (outer,)]
                    for shape, kind in coded
                ],
                pltpu.VMEM((block_rows * wide, side), F32),
                *[pltpu.VMEM((mates, HALVES) + shape, kind) for shape, kind in halved * 2],
                pltpu.VMEM((2 * inner, vecs, vecs), F32),
                pltpu.VMEM((outer * n_c, vecs, vecs), F32),
                *[pltpu.SMEM((1, slots), jnp.int32)] * 2,
                *[pltpu.VMEM((1, slots), jnp.int32)] * 2,
                dma((6,)),
                dma((TILE_COPIES,)),
                dma((GRAM + 2,)),
                dma((n_c,)),
                dma((outer * inner,)),
                dma((1,)),
                dma((1 + (inner - 1) * outer,)),
                dma((near, outer)),
                dma((outer,)),
                dma((mates, HALVES)),
                dma((2,)),
            ],
            compiler_params=pltpu.CompilerParams(
                collective_id=0, has_side_effects=True, vmem_limit_bytes=44 * 1024 * 1024
            ),
            name="arnoldi_step",
        )(
            *[
                pltpu.with_memory_space_constraint(x, pltpu.HBM)
                for x in (
                    tile_row.reshape(1, slots),
                    tile_col.reshape(1, slots),
                    right_vecs,
                    left_vecs,
                    tiles,
                )
            ]
        )
        held = [pltpu.with_memory_space_constraint(x, pltpu.VMEM) for x in held]
        return pl.pallas_call(
            flush,
            out_shape=tuple(jax.ShapeDtypeStruct(shape, F32) for shape in shapes),
            in_specs=[vmem] * len(shapes),
            out_specs=(pl.BlockSpec(memory_space=pl.ANY),) * len(shapes),
            scratch_shapes=[dma((len(shapes),))],
            name="flush",
        )(*held)

    placed = (
        P("row", "col", None, None, None),
        P("row", "col", None),
        P("row", "col", None),
        P(("row", "col"), None, None),
        P(("row", "col"), None, None),
    )
    return jax.shard_map(
        per_device,
        mesh=mesh,
        in_specs=placed,
        out_specs=(P(("row", "col"), None, None), P(("row", "col"), None, None), P()),
        check_vma=False,
    )
```

```python
import functools
from contextlib import nullcontext as scope

import jax
import jax.numpy as jnp
from jax import lax
from jax.experimental import pallas as pl
from jax.experimental.pallas import tpu as pltpu
from jax.sharding import PartitionSpec as P

MESH = pl.DeviceIdType.MESH
F32 = jnp.float32
BF16 = jnp.bfloat16
PAIR = 2
HALVES = 2
TILE_COPIES = 4
RIGHT, LEFT, PAIRED, ALONG_X, ALONG_Z, ALONG_Y, GRAM = range(7)
TOP = 32767.0
LEAST = 2.0**-110
PAD = 1


def split(value):
    high = value.astype(BF16)
    low = (value - high.astype(F32)).astype(BF16)
    return high, low


def mul(a, b, dims=(((1,), (0,)), ((), ()))):
    return lax.dot_general(a, b, dims, preferred_element_type=F32)


def flip(at, d, size):
    total, bit = 0, 1
    while bit < size:
        digit = at // bit % 2
        total = total + bit * (1 - digit if d & bit else digit)
        bit *= 2
    return total


def kernel(
    sizes,
    row_at,
    col_at,
    right,
    left,
    tiles,
    out_y,
    out_z,
    out_g,
    tbuf,
    tflip,
    cv,
    rv,
    prod,
    zp,
    zc,
    zs,
    qx_out,
    sx_out,
    qx,
    sx,
    qz_out,
    sz_out,
    qz,
    sz,
    yp,
    qy_out,
    sy_out,
    qy,
    sy,
    ga,
    gb,
    row_s,
    col_s,
    row_v,
    col_v,
    own_sem,
    tile_sem,
    send_sem,
    left_sem,
    right_sem,
    core_sem,
    zc_sem,
    zx_sem,
    zz_sem,
    zy_sem,
    g_sem,
):
    n_r, n_c, outer, inner, chunks = sizes
    piece, vecs, side = right.shape
    slots = tbuf.shape[0]
    step = slots // chunks
    block_rows = piece * n_c
    block_cols = piece * n_r
    wide = vecs + PAD
    part = piece * wide
    r = lax.axis_index("row")
    c = lax.axis_index("col")
    core = r % 2
    i = (r // 2) % inner
    o = r // (2 * inner)

    def row_of(oo, ii, cc):
        return (oo * inner + ii) * 2 + cc

    partner = (row_of(o, i, 1 - core), c)
    zs_of = [flip(o, d, outer) for d in range(outer)]
    xs_of = [flip(i, d, inner) for d in range(inner)]
    y_far = [(c + d) % n_c for d in range(1, n_c)]
    y_src = [(c - d + n_c) % n_c for d in range(1, n_c)]

    def tile_copy(ch):
        at = pl.ds(ch * (slots // TILE_COPIES), slots // TILE_COPIES)
        return pltpu.make_async_copy(tiles.at[0, 0, at], tbuf.at[at], tile_sem.at[ch])

    own = [
        pltpu.make_async_copy(src, dst, own_sem.at[q])
        for q, (src, dst) in enumerate(
            [
                (right, cv.at[pl.ds(r * piece, piece)]),
                (left, rv.at[pl.ds(c * piece, piece)]),
                (row_at, row_s),
                (col_at, col_s),
                (row_at, row_v),
                (col_at, col_v),
            ]
        )
    ]
    for copy in own:
        copy.start()
    for ch in range(TILE_COPIES):
        tile_copy(ch).start()

    barrier = pltpu.get_barrier_semaphore()
    near = [
        ((i + d) % inner, (core + e) % 2)
        for d in range(inner)
        for e in range(2)
        if d or e
    ]
    wide_set = [
        ((o + d) % outer, (c + e) % n_c)
        for d in range(outer)
        for e in range(n_c)
        if d or e
    ]
    near_peers = [(row_of(o, x, cc), c) for x, cc in near]
    wide_peers = [(row_of(z, i, core), y) for z, y in wide_set]
    peers = near_peers + wide_peers
    for peer in peers:
        pl.semaphore_signal(barrier, inc=1, device_id=peer, device_id_type=MESH)
    pl.semaphore_wait(barrier, len(peers))

    def send(src, dst, sem, peer, group):
        pltpu.make_async_remote_copy(
            src_ref=src,
            dst_ref=dst,
            send_sem=send_sem.at[group],
            recv_sem=sem,
            device_id=peer,
            device_id_type=MESH,
        ).start()

    def left_here(ref, group):
        pltpu.make_async_remote_copy(
            src_ref=ref,
            dst_ref=ref,
            send_sem=send_sem.at[group],
            recv_sem=send_sem.at[group],
            device_id=partner,
            device_id_type=MESH,
        ).wait_send()

    def landed(ref, sem):
        pltpu.make_async_remote_copy(
            src_ref=ref,
            dst_ref=ref,
            send_sem=send_sem.at[0],
            recv_sem=sem,
            device_id=partner,
            device_id_type=MESH,
        ).wait_recv()

    def cv_at(rr):
        return cv.at[pl.ds(rr * piece, piece)]

    def rv_at(cc):
        return rv.at[pl.ds(cc * piece, piece)]

    for y in y_far:
        send(left, rv_at(c), left_sem.at[c], (r, y), LEFT)
    for x in xs_of[1:]:
        send(right, cv_at(r), right_sem.at[r // 2], (row_of(o, x, core), c), RIGHT)
    for z in zs_of[1:]:
        send(right, cv_at(r), right_sem.at[r // 2], (row_of(z, i, core), c), RIGHT)
    send(right, cv_at(r), core_sem.at[0], partner, RIGHT)

    def take_z(d):
        with scope("take_z%d" % d):
            got = row_of(zs_of[d], i, core)
            landed(cv_at(got), right_sem.at[got // 2])
            for x in xs_of[1:]:
                send(cv_at(got), cv_at(got), right_sem.at[got // 2], (row_of(o, x, core), c), RIGHT)
            send(cv_at(got), cv_at(got), core_sem.at[0], partner, RIGHT)

    def take_x(d):
        with scope("take_x%d" % d):
            for x in xs_of[1:]:
                got = row_of(zs_of[d], x, core)
                landed(cv_at(got), right_sem.at[got // 2])
                send(cv_at(got), cv_at(got), core_sem.at[0], partner, RIGHT)

    def take_core():
        with scope("take_core"):
            landed(cv.at[pl.ds(0, outer * inner * piece)], core_sem.at[0])

    def turn_tiles():
        rows = lax.broadcasted_iota(jnp.int32, (side, side), 0)
        unit = rows == lax.broadcasted_iota(jnp.int32, (side, side), 1)
        unit = jnp.where(unit, 1.0, 0.0).astype(BF16)
        for ch in range(TILE_COPIES):
            with scope("wait_tiles%d" % ch):
                tile_copy(ch).wait()
            with scope("turn%d" % ch):
                part = slots // TILE_COPIES
                for s in range(ch * part, (ch + 1) * part, PAIR):
                    for q in range(PAIR):
                        tflip[s + q] = tbuf[s + q].T

    def images(first, last, tile_ref, vec_ref, index, limit):
        for s in range(first * step, last * step, PAIR):
            xs = [vec_ref[jnp.minimum(index[0, s + q], limit - 1)] for q in range(PAIR)]
            ts = [tile_ref[s + q] for q in range(PAIR)]
            got = mul(jnp.concatenate(xs, 0), jnp.concatenate(ts, 1))
            for q in range(PAIR):
                block = got[q * vecs : (q + 1) * vecs, q * side : (q + 1) * side]
                prod[pl.ds((s + q) * wide, vecs), :] = block

    across = (((1,), (1,)), ((), ()))

    def gather_sums(index_v, rows, target, first, last):
        pick = lax.broadcasted_iota(jnp.int32, (rows, slots), 0) == index_v[...]
        pick = jnp.where(pick, 1.0, 0.0).astype(BF16)
        pick = jnp.concatenate([pick, pick], 1)
        for k in range(first, last, PAIR):
            terms = [split(prod[pl.ds(k + q, slots, stride=wide), :]) for q in range(PAIR)]
            high = jnp.concatenate([t[0] for t in terms], 1)
            low = jnp.concatenate([t[1] for t in terms], 1)
            got = mul(pick, jnp.concatenate([high, low], 0))
            for q in range(PAIR):
                block = got[:, q * side : (q + 1) * side]
                target[pl.ds(k + q, rows, stride=wide), :] = block

    def encode(block_of, q_ref, s_ref, rows=vecs):
        scales = []
        for t in range(piece):
            block = block_of(t)
            top = jnp.maximum(jnp.max(jnp.abs(block), axis=0, keepdims=True), LEAST)
            q_ref[t * rows : (t + 1) * rows] = (
                jnp.round(block * (TOP / top)).astype(jnp.int32).astype(jnp.int16)
            )
            scales.append(top * (1.0 / TOP))
        s_ref[...] = jnp.concatenate(scales, 0)

    def decode(q_ref, s_ref, t, rows=vecs):
        code = q_ref[t * rows : (t + 1) * rows].astype(jnp.int32).astype(F32)
        return code * s_ref[t : t + 1]

    def post(out, dst, sem, peer, group, rows=vecs):
        codes = pl.ds(0, piece * rows)
        send(out[0].at[codes], dst[0].at[codes], sem, peer, group)
        send(out[1], dst[1], sem, peer, group)

    def pair_sum(dz, dx, t):
        at = row_of(zs_of[dz], xs_of[dx], core) * part + t * wide
        return zp[pl.ds(at, vecs), :] + zc[dx * outer + dz, t * wide : t * wide + vecs]

    merging, middle = outer == 4, (o + 1) // 2 % 2
    z_order = list(range(outer - 1, -1, -1))

    def give_core():
        with scope("give_core"):
            for dx in range(inner - 1, -1, -1):
                for dz in z_order:
                    at = pl.ds(row_of(zs_of[dz], xs_of[dx], 1 - core) * part, part)
                    slot = dx * outer + dz
                    sem = zc_sem.at[slot - outer + 1 if dx else 0]
                    send(zp.at[at], zc.at[slot], sem, partner, PAIRED)

    def paired(dz):
        for dx in range(1, inner):
            slot = dx * outer + dz
            landed(zc.at[slot], zc_sem.at[slot - outer + 1])

    def give_x(dz):
        with scope("give_x%d" % dz):
            for dx in range(inner - 1, 0, -1):
                out = qx_out.at[dx - 1, dz], sx_out.at[dx - 1, dz]
                encode(functools.partial(pair_sum, dz, dx), *out)
                peer = (row_of(o, xs_of[dx], core), c)
                dst = qx.at[dx - 1, dz], sx.at[dx - 1, dz]
                post(out, dst, zx_sem.at[dx - 1, dz], peer, ALONG_X)

    def own_x():
        with scope("own_x"):
            landed(zc.at[pl.ds(0, outer)], zc_sem.at[0])

    def plane_sum(dz, t):
        total = pair_sum(dz, 0, t)
        for d in range(1, inner):
            total = total + decode(qx.at[d - 1, dz], sx.at[d - 1, dz], t)
        return total

    def arrived(d):
        landed(qz.at[d], zz_sem.at[d])

    def encode_z(dz, extra):
        def block(t):
            total = plane_sum(dz, t)
            for d in extra:
                total = total + decode(qz.at[d], sz.at[d], t)
            return total

        encode(block, qz_out.at[dz - 1], sz_out.at[dz - 1])

    def give_z(dz, extra=()):
        with scope("give_z%d" % dz):
            for d in range(1, inner):
                landed(qx.at[d - 1, dz], zx_sem.at[d - 1, dz])
            if dz == 0:
                for t in range(piece):
                    zs[t * vecs : (t + 1) * vecs] = plane_sum(0, t)
                return
            at, z = dz - 1, zs_of[dz]
            if merging and dz == 3:
                at, z = 3 - middle, zs_of[1] + middle * (zs_of[3] - zs_of[1])
            if extra:
                arrived(extra[0])
            encode_z(dz, extra)
            out = qz_out.at[dz - 1], sz_out.at[dz - 1]
            post(out, (qz.at[at], sz.at[at]), zz_sem.at[at], (row_of(z, i, core), c), ALONG_Z)

    def gram_plane(d, total):
        with scope("gram%d" % d):
            sums, mates = [], []
            for dx in range(inner):
                p = row_of(zs_of[d], xs_of[dx], core)
                for t in range(piece):
                    high, low = split(pair_sum(d, dx, t))
                    sums.append(jnp.concatenate([high, low], 0))
                    mates.append(cv[p * piece + t])
            return total + mul(jnp.concatenate(sums, 1), jnp.concatenate(mates, 1), across)

    def spread(value, buf, stage, me, far):
        with scope("spread%d" % stage):
            buf[me] = value
            for peer in far:
                send(buf.at[me], buf.at[me], g_sem.at[stage], peer, GRAM + stage)

    def collect(buf, stage):
        with scope("collect%d" % stage):
            landed(buf.at[pl.ds(0, buf.shape[0] - 1)], g_sem.at[stage])
            total = buf[0]
            for q in range(1, buf.shape[0]):
                total = total + buf[q]
            return total

    turn_tiles()
    with scope("wait_left"):
        for copy in own:
            copy.wait()
        for y in y_src:
            landed(rv_at(y), left_sem.at[y])

    def left_images(first, last):
        with scope("imgL%d" % first):
            images(first, last, tbuf, rv, row_s, block_rows)

    def right_images(first, last):
        with scope("imgR%d" % first):
            images(first, last, tflip, cv, col_s, block_cols)

    def maybe(step, d):
        if d < outer:
            step(d)

    maybe(take_z, 1)
    left_images(0, chunks // 2)
    take_x(0)
    left_images(chunks // 2, chunks)
    maybe(take_z, 2)
    with scope("gatherZ"):
        gather_sums(col_v, block_cols, zp, 0, vecs)
    for d in range(3, outer):
        take_z(d)
    give_core()
    todo_x, todo_z = list(z_order), list(z_order)
    paired(todo_x[0])
    give_x(todo_x.pop(0))
    maybe(take_x, 1)
    for d in range(2, outer - 1):
        take_x(d)
    for d in todo_x:
        paired(d)
    while len(todo_x) > 2:
        give_x(todo_x.pop(0))
    own_x()
    total = jnp.zeros((2 * vecs, vecs), F32)
    for d in range(outer):
        if d == outer - 1 > 1:
            take_x(d)
        total = gram_plane(d, total)
    spread(total[:vecs] + total[vecs:], gb, 1, o * n_c + c, wide_peers)
    while len(todo_x) > 1:
        give_x(todo_x.pop(0))
    take_core()
    first = todo_z.pop(0)
    right_images(0, 2)
    give_z(first)
    give_x(todo_x.pop(0))
    right_images(2, chunks)

    def give_y(h):
        rows = vecs // HALVES
        with scope("gatherY%d" % h):
            gather_sums(row_v, block_rows, yp, h * rows, (h + 1) * rows)
        with scope("give_y%d" % h):
            for d, y in enumerate(y_far):
                out = qy_out.at[d, h], sy_out.at[d, h]
                start = y * part + h * rows
                encode(lambda t: yp[pl.ds(start + t * wide, rows), :], *out, rows)
                dst = qy.at[d, h], sy.at[d, h]
                post(out, dst, zy_sem.at[d, h], (r, y), ALONG_Y, rows)

    if merging:
        pl.when(middle == 0)(lambda: give_z(2))
        todo_z.remove(2)
    for h in range(HALVES):
        give_y(h)
    while len(todo_z) > 1:
        give_z(todo_z.pop(0))
    spread(collect(gb, 1), ga, 0, i * 2 + core, near_peers)
    if merging:
        pl.when(middle == 1)(lambda: give_z(2, [3]))
    give_z(0)
    gram = collect(ga, 0)
    with scope("correct"):
        gram = gram * (block_cols * n_c * side) ** (-0.5)
        out_g[...] = gram
        high, low = split(gram)
        turned_high, turned_low = split(gram.T)
        for t in range(piece):
            mine = cv[r * piece + t]
            out_y[t] = yp[pl.ds(c * part + t * wide, vecs), :] - (
                mul(turned_high, mine) + mul(turned_low, mine)
            )
            mine = rv[c * piece + t]
            out_z[t] = zs[t * vecs : (t + 1) * vecs] - (mul(high, mine) + mul(low, mine))
    for h in range(HALVES):
        rows = vecs // HALVES
        with scope("wait_y%d" % h):
            for d in range(n_c - 1):
                landed(qy.at[d, h], zy_sem.at[d, h])
        for t in range(piece):
            total = out_y[t, h * rows : (h + 1) * rows]
            for d in range(n_c - 1):
                total = total + decode(qy.at[d, h], sy.at[d, h], t, rows)
            out_y[t, h * rows : (h + 1) * rows] = total
    def add_z(slots_in):
        with scope("wait_z"):
            for d in slots_in:
                arrived(d)
        for t in range(piece):
            total = out_z[t]
            for d in slots_in:
                total = total + decode(qz.at[d], sz.at[d], t)
            out_z[t] = total

    if merging:
        pl.when(middle == 1)(lambda: add_z([0, 2, 1]))
        pl.when(middle == 0)(lambda: add_z([0, 1]))
    else:
        add_z(list(range(outer - 1)))
    with scope("wait_send"):
        left_here(cv.at[pl.ds(0, (n_r - 1) * piece)], RIGHT)
        left_here(rv.at[pl.ds(0, (n_c - 1) * piece)], LEFT)
        left_here(zc, PAIRED)
        left_here(qx_out, ALONG_X)
        left_here(qz_out, ALONG_Z)
        left_here(qy_out, ALONG_Y)
        left_here(ga.at[pl.ds(0, 2 * inner - 1)], GRAM)
        left_here(gb.at[pl.ds(0, outer * n_c - 1)], GRAM + 1)


def flush(*refs):
    sem = refs[-1]
    half = len(refs) // 2
    copies = [
        pltpu.make_async_copy(refs[q], refs[half + q], sem.at[q]) for q in range(half)
    ]
    for copy in copies:
        copy.start()
    for copy in copies:
        copy.wait()


def solution(mesh):
    n_r, n_c = mesh.shape["row"], mesh.shape["col"]
    half = n_r // 2
    inner = 1 << ((half.bit_length() - 1) // 2)
    outer = half // inner

    def per_device(tiles, tile_row, tile_col, right_vecs, left_vecs):
        slots, side = tiles.shape[2], tiles.shape[3]
        piece, vecs, _ = right_vecs.shape
        chunks = 8
        wide = vecs + PAD
        part = piece * wide
        block_rows, block_cols = piece * n_c, piece * n_r
        planes = outer * inner
        near, far, mates = max(inner - 1, 1), max(outer - 1, 1), max(n_c - 1, 1)
        rows = vecs // HALVES
        coded = [((piece * (vecs + 2), side), jnp.int16), ((piece, side), F32)]
        halved = [((piece * (rows + 2), side), jnp.int16), ((piece, side), F32)]
        vmem = pl.BlockSpec(memory_space=pltpu.VMEM)
        dma = pltpu.SemaphoreType.DMA
        shapes = [(piece, vecs, side), (piece, vecs, side), (vecs, vecs)]
        held = pl.pallas_call(
            functools.partial(kernel, (n_r, n_c, outer, inner, chunks)),
            out_shape=tuple(pltpu.VMEM(shape, F32) for shape in shapes),
            in_specs=[pl.BlockSpec(memory_space=pltpu.HBM)] * 5,
            out_specs=(vmem, vmem, vmem),
            scratch_shapes=[
                pltpu.VMEM((slots, side, side), BF16),
                pltpu.VMEM((slots, side, side), BF16),
                pltpu.VMEM((block_cols, vecs, side), BF16),
                pltpu.VMEM((block_rows, vecs, side), BF16),
                pltpu.VMEM((slots * wide, side), F32),
                pltpu.VMEM((block_cols * wide, side), F32),
                pltpu.VMEM((planes, part, side), F32),
                pltpu.VMEM((piece * vecs, side), F32),
                *[
                    pltpu.VMEM(lead + shape, kind)
                    for lead in [(near, outer)] * 2 + [(far,), (outer,)]
                    for shape, kind in coded
                ],
                pltpu.VMEM((block_rows * wide, side), F32),
                *[pltpu.VMEM((mates, HALVES) + shape, kind) for shape, kind in halved * 2],
                pltpu.VMEM((2 * inner, vecs, vecs), F32),
                pltpu.VMEM((outer * n_c, vecs, vecs), F32),
                *[pltpu.SMEM((1, slots), jnp.int32)] * 2,
                *[pltpu.VMEM((1, slots), jnp.int32)] * 2,
                dma((6,)),
                dma((TILE_COPIES,)),
                dma((GRAM + 2,)),
                dma((n_c,)),
                dma((outer * inner,)),
                dma((1,)),
                dma((1 + (inner - 1) * outer,)),
                dma((near, outer)),
                dma((outer,)),
                dma((mates, HALVES)),
                dma((2,)),
            ],
            compiler_params=pltpu.CompilerParams(
                collective_id=0, has_side_effects=True, vmem_limit_bytes=44 * 1024 * 1024
            ),
            name="arnoldi_step",
        )(
            *[
                pltpu.with_memory_space_constraint(x, pltpu.HBM)
                for x in (
                    tile_row.reshape(1, slots),
                    tile_col.reshape(1, slots),
                    right_vecs,
                    left_vecs,
                    tiles,
                )
            ]
        )
        held = [pltpu.with_memory_space_constraint(x, pltpu.VMEM) for x in held]
        return pl.pallas_call(
            flush,
            out_shape=tuple(jax.ShapeDtypeStruct(shape, F32) for shape in shapes),
            in_specs=[vmem] * len(shapes),
            out_specs=(pl.BlockSpec(memory_space=pl.ANY),) * len(shapes),
            scratch_shapes=[dma((len(shapes),))],
            name="flush",
        )(*held)

    placed = (
        P("row", "col", None, None, None),
        P("row", "col", None),
        P("row", "col", None),
        P(("row", "col"), None, None),
        P(("row", "col"), None, None),
    )
    return jax.shard_map(
        per_device,
        mesh=mesh,
        in_specs=placed,
        out_specs=(P(("row", "col"), None, None), P(("row", "col"), None, None), P()),
        check_vma=False,
    )
```

```python
import functools
from contextlib import nullcontext as scope

import jax
import jax.numpy as jnp
from jax import lax
from jax.experimental import pallas as pl
from jax.experimental.pallas import tpu as pltpu
from jax.sharding import PartitionSpec as P

MESH = pl.DeviceIdType.MESH
F32 = jnp.float32
BF16 = jnp.bfloat16
PAIR = 2
HALVES = 2
TILE_COPIES = 4
RIGHT, LEFT, PAIRED, ALONG_X, ALONG_Z, ALONG_Y, GRAM = range(7)
TOP = 32767.0
LEAST = 2.0**-110
PAD = 1


def split(value):
    high = value.astype(BF16)
    low = (value - high.astype(F32)).astype(BF16)
    return high, low


def mul(a, b, dims=(((1,), (0,)), ((), ()))):
    return lax.dot_general(a, b, dims, preferred_element_type=F32)


def flip(at, d, size):
    total, bit = 0, 1
    while bit < size:
        digit = at // bit % 2
        total = total + bit * (1 - digit if d & bit else digit)
        bit *= 2
    return total


def kernel(
    sizes,
    row_at,
    col_at,
    right,
    left,
    tiles,
    out_y,
    out_z,
    out_g,
    tbuf,
    tflip,
    cv,
    rv,
    prod,
    zp,
    zc,
    zs,
    qx_out,
    sx_out,
    qx,
    sx,
    qz_out,
    sz_out,
    qz,
    sz,
    yp,
    qy_out,
    sy_out,
    qy,
    sy,
    ga,
    gb,
    row_s,
    col_s,
    row_v,
    col_v,
    own_sem,
    tile_sem,
    send_sem,
    left_sem,
    right_sem,
    core_sem,
    zc_sem,
    zx_sem,
    zz_sem,
    zy_sem,
    g_sem,
):
    n_r, n_c, outer, inner, chunks = sizes
    piece, vecs, side = right.shape
    slots = tbuf.shape[0]
    step = slots // chunks
    block_rows = piece * n_c
    block_cols = piece * n_r
    wide = vecs + PAD
    part = piece * wide
    r = lax.axis_index("row")
    c = lax.axis_index("col")
    core = r % 2
    i = (r // 2) % inner
    o = r // (2 * inner)

    def row_of(oo, ii, cc):
        return (oo * inner + ii) * 2 + cc

    partner = (row_of(o, i, 1 - core), c)
    zs_of = [flip(o, d, outer) for d in range(outer)]
    xs_of = [flip(i, d, inner) for d in range(inner)]
    y_far = [(c + d) % n_c for d in range(1, n_c)]
    y_src = [(c - d + n_c) % n_c for d in range(1, n_c)]

    def tile_copy(ch):
        at = pl.ds(ch * (slots // TILE_COPIES), slots // TILE_COPIES)
        return pltpu.make_async_copy(tiles.at[0, 0, at], tbuf.at[at], tile_sem.at[ch])

    own = [
        pltpu.make_async_copy(src, dst, own_sem.at[q])
        for q, (src, dst) in enumerate(
            [
                (right, cv.at[pl.ds(r * piece, piece)]),
                (left, rv.at[pl.ds(c * piece, piece)]),
                (row_at, row_s),
                (col_at, col_s),
                (row_at, row_v),
                (col_at, col_v),
            ]
        )
    ]
    for copy in own:
        copy.start()
    for ch in range(TILE_COPIES):
        tile_copy(ch).start()

    barrier = pltpu.get_barrier_semaphore()
    near = [
        ((i + d) % inner, (core + e) % 2)
        for d in range(inner)
        for e in range(2)
        if d or e
    ]
    wide_set = [
        ((o + d) % outer, (c + e) % n_c)
        for d in range(outer)
        for e in range(n_c)
        if d or e
    ]
    near_peers = [(row_of(o, x, cc), c) for x, cc in near]
    wide_peers = [(row_of(z, i, core), y) for z, y in wide_set]
    peers = near_peers + wide_peers
    for peer in peers:
        pl.semaphore_signal(barrier, inc=1, device_id=peer, device_id_type=MESH)
    pl.semaphore_wait(barrier, len(peers))

    def send(src, dst, sem, peer, group):
        pltpu.make_async_remote_copy(
            src_ref=src,
            dst_ref=dst,
            send_sem=send_sem.at[group],
            recv_sem=sem,
            device_id=peer,
            device_id_type=MESH,
        ).start()

    def left_here(ref, group):
        pltpu.make_async_remote_copy(
            src_ref=ref,
            dst_ref=ref,
            send_sem=send_sem.at[group],
            recv_sem=send_sem.at[group],
            device_id=partner,
            device_id_type=MESH,
        ).wait_send()

    def landed(ref, sem):
        pltpu.make_async_remote_copy(
            src_ref=ref,
            dst_ref=ref,
            send_sem=send_sem.at[0],
            recv_sem=sem,
            device_id=partner,
            device_id_type=MESH,
        ).wait_recv()

    def cv_at(rr):
        return cv.at[pl.ds(rr * piece, piece)]

    def rv_at(cc):
        return rv.at[pl.ds(cc * piece, piece)]

    for y in y_far:
        send(left, rv_at(c), left_sem.at[c], (r, y), LEFT)
    for x in xs_of[1:]:
        send(right, cv_at(r), right_sem.at[r // 2], (row_of(o, x, core), c), RIGHT)
    for z in zs_of[1:]:
        send(right, cv_at(r), right_sem.at[r // 2], (row_of(z, i, core), c), RIGHT)
    send(right, cv_at(r), core_sem.at[0], partner, RIGHT)

    def take_z(d):
        with scope("take_z%d" % d):
            got = row_of(zs_of[d], i, core)
            landed(cv_at(got), right_sem.at[got // 2])
            for x in xs_of[1:]:
                send(cv_at(got), cv_at(got), right_sem.at[got // 2], (row_of(o, x, core), c), RIGHT)
            send(cv_at(got), cv_at(got), core_sem.at[0], partner, RIGHT)

    def take_x(d):
        with scope("take_x%d" % d):
            for x in xs_of[1:]:
                got = row_of(zs_of[d], x, core)
                landed(cv_at(got), right_sem.at[got // 2])
                send(cv_at(got), cv_at(got), core_sem.at[0], partner, RIGHT)

    def take_core():
        with scope("take_core"):
            landed(cv.at[pl.ds(0, outer * inner * piece)], core_sem.at[0])

    def turn_tiles():
        rows = lax.broadcasted_iota(jnp.int32, (side, side), 0)
        unit = rows == lax.broadcasted_iota(jnp.int32, (side, side), 1)
        unit = jnp.where(unit, 1.0, 0.0).astype(BF16)
        for ch in range(TILE_COPIES):
            with scope("wait_tiles%d" % ch):
                tile_copy(ch).wait()
            with scope("turn%d" % ch):
                part = slots // TILE_COPIES
                for s in range(ch * part, (ch + 1) * part, PAIR):
                    for q in range(PAIR):
                        tflip[s + q] = tbuf[s + q].T

    def images(first, last, tile_ref, vec_ref, index, limit):
        for s in range(first * step, last * step, PAIR):
            xs = [vec_ref[jnp.minimum(index[0, s + q], limit - 1)] for q in range(PAIR)]
            ts = [tile_ref[s + q] for q in range(PAIR)]
            got = mul(jnp.concatenate(xs, 0), jnp.concatenate(ts, 1))
            for q in range(PAIR):
                block = got[q * vecs : (q + 1) * vecs, q * side : (q + 1) * side]
                prod[pl.ds((s + q) * wide, vecs), :] = block

    across = (((1,), (1,)), ((), ()))

    def gather_sums(index_v, rows, target, first, last):
        pick = lax.broadcasted_iota(jnp.int32, (rows, slots), 0) == index_v[...]
        pick = jnp.where(pick, 1.0, 0.0).astype(BF16)
        pick = jnp.concatenate([pick, pick], 1)
        for k in range(first, last, PAIR):
            terms = [split(prod[pl.ds(k + q, slots, stride=wide), :]) for q in range(PAIR)]
            high = jnp.concatenate([t[0] for t in terms], 1)
            low = jnp.concatenate([t[1] for t in terms], 1)
            got = mul(pick, jnp.concatenate([high, low], 0))
            for q in range(PAIR):
                block = got[:, q * side : (q + 1) * side]
                target[pl.ds(k + q, rows, stride=wide), :] = block

    def encode(block_of, q_ref, s_ref, rows=vecs):
        scales = []
        for t in range(piece):
            block = block_of(t)
            top = jnp.maximum(jnp.max(jnp.abs(block), axis=0, keepdims=True), LEAST)
            q_ref[t * rows : (t + 1) * rows] = (
                jnp.round(block * (TOP / top)).astype(jnp.int32).astype(jnp.int16)
            )
            scales.append(top * (1.0 / TOP))
        s_ref[...] = jnp.concatenate(scales, 0)

    def decode(q_ref, s_ref, t, rows=vecs):
        code = q_ref[t * rows : (t + 1) * rows].astype(jnp.int32).astype(F32)
        return code * s_ref[t : t + 1]

    def post(out, dst, sem, peer, group, rows=vecs):
        codes = pl.ds(0, piece * rows)
        send(out[0].at[codes], dst[0].at[codes], sem, peer, group)
        send(out[1], dst[1], sem, peer, group)

    def pair_sum(dz, dx, t):
        at = row_of(zs_of[dz], xs_of[dx], core) * part + t * wide
        return zp[pl.ds(at, vecs), :] + zc[dx * outer + dz, t * wide : t * wide + vecs]

    merging, middle = outer == 4, (o + 1) // 2 % 2
    z_order = list(range(outer - 1, -1, -1))

    def give_core():
        with scope("give_core"):
            for dx in range(inner - 1, -1, -1):
                for dz in z_order:
                    at = pl.ds(row_of(zs_of[dz], xs_of[dx], 1 - core) * part, part)
                    slot = dx * outer + dz
                    sem = zc_sem.at[slot - outer + 1 if dx else 0]
                    send(zp.at[at], zc.at[slot], sem, partner, PAIRED)

    def paired(dz):
        for dx in range(1, inner):
            slot = dx * outer + dz
            landed(zc.at[slot], zc_sem.at[slot - outer + 1])

    def give_x(dz):
        with scope("give_x%d" % dz):
            for dx in range(inner - 1, 0, -1):
                out = qx_out.at[dx - 1, dz], sx_out.at[dx - 1, dz]
                encode(functools.partial(pair_sum, dz, dx), *out)
                peer = (row_of(o, xs_of[dx], core), c)
                dst = qx.at[dx - 1, dz], sx.at[dx - 1, dz]
                post(out, dst, zx_sem.at[dx - 1, dz], peer, ALONG_X)

    def own_x():
        with scope("own_x"):
            landed(zc.at[pl.ds(0, outer)], zc_sem.at[0])

    def plane_sum(dz, t):
        total = pair_sum(dz, 0, t)
        for d in range(1, inner):
            total = total + decode(qx.at[d - 1, dz], sx.at[d - 1, dz], t)
        return total

    def arrived(d):
        landed(qz.at[d], zz_sem.at[d])

    def encode_z(dz, extra):
        def block(t):
            total = plane_sum(dz, t)
            for d in extra:
                total = total + decode(qz.at[d], sz.at[d], t)
            return total

        encode(block, qz_out.at[dz - 1], sz_out.at[dz - 1])

    def give_z(dz, extra=()):
        with scope("give_z%d" % dz):
            for d in range(1, inner):
                landed(qx.at[d - 1, dz], zx_sem.at[d - 1, dz])
            if dz == 0:
                for t in range(piece):
                    zs[t * vecs : (t + 1) * vecs] = plane_sum(0, t)
                return
            at, z = dz - 1, zs_of[dz]
            if merging and dz == 3:
                at, z = 3 - middle, zs_of[1] + middle * (zs_of[3] - zs_of[1])
            if extra:
                arrived(extra[0])
            encode_z(dz, extra)
            out = qz_out.at[dz - 1], sz_out.at[dz - 1]
            post(out, (qz.at[at], sz.at[at]), zz_sem.at[at], (row_of(z, i, core), c), ALONG_Z)

    def gram_plane(d, total):
        with scope("gram%d" % d):
            sums, mates = [], []
            for dx in range(inner):
                p = row_of(zs_of[d], xs_of[dx], core)
                for t in range(piece):
                    high, low = split(pair_sum(d, dx, t))
                    sums.append(jnp.concatenate([high, low], 0))
                    mates.append(cv[p * piece + t])
            return total + mul(jnp.concatenate(sums, 1), jnp.concatenate(mates, 1), across)

    def spread(value, buf, stage, me, far):
        with scope("spread%d" % stage):
            buf[me] = value
            for peer in far:
                send(buf.at[me], buf.at[me], g_sem.at[stage], peer, GRAM + stage)

    def collect(buf, stage):
        with scope("collect%d" % stage):
            landed(buf.at[pl.ds(0, buf.shape[0] - 1)], g_sem.at[stage])
            total = buf[0]
            for q in range(1, buf.shape[0]):
                total = total + buf[q]
            return total

    turn_tiles()
    with scope("wait_left"):
        for copy in own:
            copy.wait()
        for y in y_src:
            landed(rv_at(y), left_sem.at[y])

    def left_images(first, last):
        with scope("imgL%d" % first):
            images(first, last, tbuf, rv, row_s, block_rows)

    def right_images(first, last):
        with scope("imgR%d" % first):
            images(first, last, tflip, cv, col_s, block_cols)

    def maybe(step, d):
        if d < outer:
            step(d)

    left_images(0, 2)
    maybe(take_z, 1)
    left_images(2, chunks)
    take_x(0)
    maybe(take_z, 2)
    with scope("gatherZ"):
        gather_sums(col_v, block_cols, zp, 0, vecs)
    for d in range(3, outer):
        take_z(d)
    give_core()
    todo_x, todo_z = list(z_order), list(z_order)
    paired(todo_x[0])
    give_x(todo_x.pop(0))
    maybe(take_x, 1)
    for d in range(2, outer - 1):
        take_x(d)
    for d in todo_x:
        paired(d)
    while len(todo_x) > 2:
        give_x(todo_x.pop(0))
    own_x()
    total = jnp.zeros((2 * vecs, vecs), F32)
    for d in range(outer):
        if d == outer - 1 > 1:
            take_x(d)
        total = gram_plane(d, total)
    spread(total[:vecs] + total[vecs:], gb, 1, o * n_c + c, wide_peers)
    while len(todo_x) > 1:
        give_x(todo_x.pop(0))
    take_core()
    first = todo_z.pop(0)
    right_images(0, 2)
    give_z(first)
    give_x(todo_x.pop(0))
    right_images(2, chunks)

    def give_y(h):
        rows = vecs // HALVES
        with scope("gatherY%d" % h):
            gather_sums(row_v, block_rows, yp, h * rows, (h + 1) * rows)
        with scope("give_y%d" % h):
            for d, y in enumerate(y_far):
                out = qy_out.at[d, h], sy_out.at[d, h]
                start = y * part + h * rows
                encode(lambda t: yp[pl.ds(start + t * wide, rows), :], *out, rows)
                dst = qy.at[d, h], sy.at[d, h]
                post(out, dst, zy_sem.at[d, h], (r, y), ALONG_Y, rows)

    if merging:
        pl.when(middle == 0)(lambda: give_z(2))
        todo_z.remove(2)
    for h in range(HALVES):
        give_y(h)
    while len(todo_z) > 1:
        give_z(todo_z.pop(0))
    spread(collect(gb, 1), ga, 0, i * 2 + core, near_peers)
    if merging:
        pl.when(middle == 1)(lambda: give_z(2, [3]))
    give_z(0)
    gram = collect(ga, 0)
    with scope("correct"):
        gram = gram * (block_cols * n_c * side) ** (-0.5)
        out_g[...] = gram
        high, low = split(gram)
        turned_high, turned_low = split(gram.T)
        for t in range(piece):
            mine = cv[r * piece + t]
            out_y[t] = yp[pl.ds(c * part + t * wide, vecs), :] - (
                mul(turned_high, mine) + mul(turned_low, mine)
            )
            mine = rv[c * piece + t]
            out_z[t] = zs[t * vecs : (t + 1) * vecs] - (mul(high, mine) + mul(low, mine))
    for h in range(HALVES):
        rows = vecs // HALVES
        with scope("wait_y%d" % h):
            for d in range(n_c - 1):
                landed(qy.at[d, h], zy_sem.at[d, h])
        for t in range(piece):
            total = out_y[t, h * rows : (h + 1) * rows]
            for d in range(n_c - 1):
                total = total + decode(qy.at[d, h], sy.at[d, h], t, rows)
            out_y[t, h * rows : (h + 1) * rows] = total
    def add_z(slots_in):
        with scope("wait_z"):
            for d in slots_in:
                arrived(d)
        for t in range(piece):
            total = out_z[t]
            for d in slots_in:
                total = total + decode(qz.at[d], sz.at[d], t)
            out_z[t] = total

    if merging:
        pl.when(middle == 1)(lambda: add_z([0, 2, 1]))
        pl.when(middle == 0)(lambda: add_z([0, 1]))
    else:
        add_z(list(range(outer - 1)))
    with scope("wait_send"):
        left_here(cv.at[pl.ds(0, (n_r - 1) * piece)], RIGHT)
        left_here(rv.at[pl.ds(0, (n_c - 1) * piece)], LEFT)
        left_here(zc, PAIRED)
        left_here(qx_out, ALONG_X)
        left_here(qz_out, ALONG_Z)
        left_here(qy_out, ALONG_Y)
        left_here(ga.at[pl.ds(0, 2 * inner - 1)], GRAM)
        left_here(gb.at[pl.ds(0, outer * n_c - 1)], GRAM + 1)


def flush(*refs):
    sem = refs[-1]
    half = len(refs) // 2
    copies = [
        pltpu.make_async_copy(refs[q], refs[half + q], sem.at[q]) for q in range(half)
    ]
    for copy in copies:
        copy.start()
    for copy in copies:
        copy.wait()


def solution(mesh):
    n_r, n_c = mesh.shape["row"], mesh.shape["col"]
    half = n_r // 2
    inner = 1 << ((half.bit_length() - 1) // 2)
    outer = half // inner

    def per_device(tiles, tile_row, tile_col, right_vecs, left_vecs):
        slots, side = tiles.shape[2], tiles.shape[3]
        piece, vecs, _ = right_vecs.shape
        chunks = 8
        wide = vecs + PAD
        part = piece * wide
        block_rows, block_cols = piece * n_c, piece * n_r
        planes = outer * inner
        near, far, mates = max(inner - 1, 1), max(outer - 1, 1), max(n_c - 1, 1)
        rows = vecs // HALVES
        coded = [((piece * (vecs + 2), side), jnp.int16), ((piece, side), F32)]
        halved = [((piece * (rows + 2), side), jnp.int16), ((piece, side), F32)]
        vmem = pl.BlockSpec(memory_space=pltpu.VMEM)
        dma = pltpu.SemaphoreType.DMA
        shapes = [(piece, vecs, side), (piece, vecs, side), (vecs, vecs)]
        held = pl.pallas_call(
            functools.partial(kernel, (n_r, n_c, outer, inner, chunks)),
            out_shape=tuple(pltpu.VMEM(shape, F32) for shape in shapes),
            in_specs=[pl.BlockSpec(memory_space=pltpu.HBM)] * 5,
            out_specs=(vmem, vmem, vmem),
            scratch_shapes=[
                pltpu.VMEM((slots, side, side), BF16),
                pltpu.VMEM((slots, side, side), BF16),
                pltpu.VMEM((block_cols, vecs, side), BF16),
                pltpu.VMEM((block_rows, vecs, side), BF16),
                pltpu.VMEM((slots * wide, side), F32),
                pltpu.VMEM((block_cols * wide, side), F32),
                pltpu.VMEM((planes, part, side), F32),
                pltpu.VMEM((piece * vecs, side), F32),
                *[
                    pltpu.VMEM(lead + shape, kind)
                    for lead in [(near, outer)] * 2 + [(far,), (outer,)]
                    for shape, kind in coded
                ],
                pltpu.VMEM((block_rows * wide, side), F32),
                *[pltpu.VMEM((mates, HALVES) + shape, kind) for shape, kind in halved * 2],
                pltpu.VMEM((2 * inner, vecs, vecs), F32),
                pltpu.VMEM((outer * n_c, vecs, vecs), F32),
                *[pltpu.SMEM((1, slots), jnp.int32)] * 2,
                *[pltpu.VMEM((1, slots), jnp.int32)] * 2,
                dma((6,)),
                dma((TILE_COPIES,)),
                dma((GRAM + 2,)),
                dma((n_c,)),
                dma((outer * inner,)),
                dma((1,)),
                dma((1 + (inner - 1) * outer,)),
                dma((near, outer)),
                dma((outer,)),
                dma((mates, HALVES)),
                dma((2,)),
            ],
            compiler_params=pltpu.CompilerParams(
                collective_id=0, has_side_effects=True, vmem_limit_bytes=44 * 1024 * 1024
            ),
            name="arnoldi_step",
        )(
            *[
                pltpu.with_memory_space_constraint(x, pltpu.HBM)
                for x in (
                    tile_row.reshape(1, slots),
                    tile_col.reshape(1, slots),
                    right_vecs,
                    left_vecs,
                    tiles,
                )
            ]
        )
        held = [pltpu.with_memory_space_constraint(x, pltpu.VMEM) for x in held]
        return pl.pallas_call(
            flush,
            out_shape=tuple(jax.ShapeDtypeStruct(shape, F32) for shape in shapes),
            in_specs=[vmem] * len(shapes),
            out_specs=(pl.BlockSpec(memory_space=pl.ANY),) * len(shapes),
            scratch_shapes=[dma((len(shapes),))],
            name="flush",
        )(*held)

    placed = (
        P("row", "col", None, None, None),
        P("row", "col", None),
        P("row", "col", None),
        P(("row", "col"), None, None),
        P(("row", "col"), None, None),
    )
    return jax.shard_map(
        per_device,
        mesh=mesh,
        in_specs=placed,
        out_specs=(P(("row", "col"), None, None), P(("row", "col"), None, None), P()),
        check_vma=False,
    )
```

```python
import functools
from contextlib import nullcontext as scope

import jax
import jax.numpy as jnp
from jax import lax
from jax.experimental import pallas as pl
from jax.experimental.pallas import tpu as pltpu
from jax.sharding import PartitionSpec as P

MESH = pl.DeviceIdType.MESH
F32 = jnp.float32
BF16 = jnp.bfloat16
PAIR = 2
HALVES = 2
TILE_COPIES = 4
RIGHT, LEFT, PAIRED, ALONG_X, ALONG_Z, ALONG_Y, GRAM = range(7)
TOP = 32767.0
LEAST = 2.0**-110
PAD = 1


def split(value):
    high = value.astype(BF16)
    low = (value - high.astype(F32)).astype(BF16)
    return high, low


def mul(a, b, dims=(((1,), (0,)), ((), ()))):
    return lax.dot_general(a, b, dims, preferred_element_type=F32)


def flip(at, d, size):
    total, bit = 0, 1
    while bit < size:
        digit = at // bit % 2
        total = total + bit * (1 - digit if d & bit else digit)
        bit *= 2
    return total


def kernel(
    sizes,
    row_at,
    col_at,
    right,
    left,
    tiles,
    out_y,
    out_z,
    out_g,
    tbuf,
    tflip,
    cv,
    rv,
    prod,
    zp,
    zc,
    zs,
    qx_out,
    sx_out,
    qx,
    sx,
    qz_out,
    sz_out,
    qz,
    sz,
    yp,
    qy_out,
    sy_out,
    qy,
    sy,
    ga,
    gb,
    row_s,
    col_s,
    row_v,
    col_v,
    own_sem,
    tile_sem,
    send_sem,
    left_sem,
    right_sem,
    core_sem,
    zc_sem,
    zx_sem,
    zz_sem,
    zy_sem,
    g_sem,
):
    n_r, n_c, outer, inner, chunks = sizes
    piece, vecs, side = right.shape
    slots = tbuf.shape[0]
    step = slots // chunks
    block_rows = piece * n_c
    block_cols = piece * n_r
    wide = vecs + PAD
    part = piece * wide
    r = lax.axis_index("row")
    c = lax.axis_index("col")
    core = r % 2
    i = (r // 2) % inner
    o = r // (2 * inner)

    def row_of(oo, ii, cc):
        return (oo * inner + ii) * 2 + cc

    partner = (row_of(o, i, 1 - core), c)
    zs_of = [flip(o, d, outer) for d in range(outer)]
    xs_of = [flip(i, d, inner) for d in range(inner)]
    y_far = [(c + d) % n_c for d in range(1, n_c)]
    y_src = [(c - d + n_c) % n_c for d in range(1, n_c)]

    def tile_copy(ch):
        at = pl.ds(ch * (slots // TILE_COPIES), slots // TILE_COPIES)
        return pltpu.make_async_copy(tiles.at[0, 0, at], tbuf.at[at], tile_sem.at[ch])

    own = [
        pltpu.make_async_copy(src, dst, own_sem.at[q])
        for q, (src, dst) in enumerate(
            [
                (right, cv.at[pl.ds(r * piece, piece)]),
                (left, rv.at[pl.ds(c * piece, piece)]),
                (row_at, row_s),
                (col_at, col_s),
                (row_at, row_v),
                (col_at, col_v),
            ]
        )
    ]
    for copy in own:
        copy.start()
    for ch in range(TILE_COPIES):
        tile_copy(ch).start()

    barrier = pltpu.get_barrier_semaphore()
    near = [
        ((i + d) % inner, (core + e) % 2)
        for d in range(inner)
        for e in range(2)
        if d or e
    ]
    wide_set = [
        ((o + d) % outer, (c + e) % n_c)
        for d in range(outer)
        for e in range(n_c)
        if d or e
    ]
    near_peers = [(row_of(o, x, cc), c) for x, cc in near]
    wide_peers = [(row_of(z, i, core), y) for z, y in wide_set]
    peers = near_peers + wide_peers
    for peer in peers:
        pl.semaphore_signal(barrier, inc=1, device_id=peer, device_id_type=MESH)
    pl.semaphore_wait(barrier, len(peers))

    def send(src, dst, sem, peer, group):
        pltpu.make_async_remote_copy(
            src_ref=src,
            dst_ref=dst,
            send_sem=send_sem.at[group],
            recv_sem=sem,
            device_id=peer,
            device_id_type=MESH,
        ).start()

    def left_here(ref, group):
        pltpu.make_async_remote_copy(
            src_ref=ref,
            dst_ref=ref,
            send_sem=send_sem.at[group],
            recv_sem=send_sem.at[group],
            device_id=partner,
            device_id_type=MESH,
        ).wait_send()

    def landed(ref, sem):
        pltpu.make_async_remote_copy(
            src_ref=ref,
            dst_ref=ref,
            send_sem=send_sem.at[0],
            recv_sem=sem,
            device_id=partner,
            device_id_type=MESH,
        ).wait_recv()

    def cv_at(rr):
        return cv.at[pl.ds(rr * piece, piece)]

    def rv_at(cc):
        return rv.at[pl.ds(cc * piece, piece)]

    for y in y_far:
        send(left, rv_at(c), left_sem.at[c], (r, y), LEFT)
    for x in xs_of[1:]:
        send(right, cv_at(r), right_sem.at[r // 2], (row_of(o, x, core), c), RIGHT)
    for z in zs_of[1:]:
        send(right, cv_at(r), right_sem.at[r // 2], (row_of(z, i, core), c), RIGHT)
    send(right, cv_at(r), core_sem.at[0], partner, RIGHT)

    def take_z(d):
        with scope("take_z%d" % d):
            got = row_of(zs_of[d], i, core)
            landed(cv_at(got), right_sem.at[got // 2])
            for x in xs_of[1:]:
                send(cv_at(got), cv_at(got), right_sem.at[got // 2], (row_of(o, x, core), c), RIGHT)
            send(cv_at(got), cv_at(got), core_sem.at[0], partner, RIGHT)

    def take_x(d):
        with scope("take_x%d" % d):
            for x in xs_of[1:]:
                got = row_of(zs_of[d], x, core)
                landed(cv_at(got), right_sem.at[got // 2])
                send(cv_at(got), cv_at(got), core_sem.at[0], partner, RIGHT)

    def take_core():
        with scope("take_core"):
            landed(cv.at[pl.ds(0, outer * inner * piece)], core_sem.at[0])

    def turn_tiles():
        rows = lax.broadcasted_iota(jnp.int32, (side, side), 0)
        unit = rows == lax.broadcasted_iota(jnp.int32, (side, side), 1)
        unit = jnp.where(unit, 1.0, 0.0).astype(BF16)
        for ch in range(TILE_COPIES):
            with scope("wait_tiles%d" % ch):
                tile_copy(ch).wait()
            with scope("turn%d" % ch):
                part = slots // TILE_COPIES
                for s in range(ch * part, (ch + 1) * part, PAIR):
                    for q in range(PAIR):
                        tflip[s + q] = tbuf[s + q].T

    def images(first, last, tile_ref, vec_ref, index, limit):
        for s in range(first * step, last * step, PAIR):
            xs = [vec_ref[jnp.minimum(index[0, s + q], limit - 1)] for q in range(PAIR)]
            ts = [tile_ref[s + q] for q in range(PAIR)]
            got = mul(jnp.concatenate(xs, 0), jnp.concatenate(ts, 1))
            for q in range(PAIR):
                block = got[q * vecs : (q + 1) * vecs, q * side : (q + 1) * side]
                prod[pl.ds((s + q) * wide, vecs), :] = block

    across = (((1,), (1,)), ((), ()))

    def gather_sums(index_v, rows, target, first, last):
        pick = lax.broadcasted_iota(jnp.int32, (rows, slots), 0) == index_v[...]
        pick = jnp.where(pick, 1.0, 0.0).astype(BF16)
        pick = jnp.concatenate([pick, pick], 1)
        for k in range(first, last, PAIR):
            terms = [split(prod[pl.ds(k + q, slots, stride=wide), :]) for q in range(PAIR)]
            high = jnp.concatenate([t[0] for t in terms], 1)
            low = jnp.concatenate([t[1] for t in terms], 1)
            got = mul(pick, jnp.concatenate([high, low], 0))
            for q in range(PAIR):
                block = got[:, q * side : (q + 1) * side]
                target[pl.ds(k + q, rows, stride=wide), :] = block

    def encode(block_of, q_ref, s_ref, rows=vecs):
        scales = []
        for t in range(piece):
            block = block_of(t)
            top = jnp.maximum(jnp.max(jnp.abs(block), axis=0, keepdims=True), LEAST)
            q_ref[t * rows : (t + 1) * rows] = (
                jnp.round(block * (TOP / top)).astype(jnp.int32).astype(jnp.int16)
            )
            scales.append(top * (1.0 / TOP))
        s_ref[...] = jnp.concatenate(scales, 0)

    def decode(q_ref, s_ref, t, rows=vecs):
        code = q_ref[t * rows : (t + 1) * rows].astype(jnp.int32).astype(F32)
        return code * s_ref[t : t + 1]

    def post(out, dst, sem, peer, group, rows=vecs):
        codes = pl.ds(0, piece * rows)
        send(out[0].at[codes], dst[0].at[codes], sem, peer, group)
        send(out[1], dst[1], sem, peer, group)

    def pair_sum(dz, dx, t):
        at = row_of(zs_of[dz], xs_of[dx], core) * part + t * wide
        return zp[pl.ds(at, vecs), :] + zc[dx * outer + dz, t * wide : t * wide + vecs]

    merging, middle = outer == 4, (o + 1) // 2 % 2
    z_order = list(range(outer - 1, -1, -1))

    def give_core():
        with scope("give_core"):
            for dx in range(inner - 1, -1, -1):
                for dz in z_order:
                    at = pl.ds(row_of(zs_of[dz], xs_of[dx], 1 - core) * part, part)
                    slot = dx * outer + dz
                    sem = zc_sem.at[slot - outer + 1 if dx else 0]
                    send(zp.at[at], zc.at[slot], sem, partner, PAIRED)

    def paired(dz):
        for dx in range(1, inner):
            slot = dx * outer + dz
            landed(zc.at[slot], zc_sem.at[slot - outer + 1])

    def give_x(dz):
        with scope("give_x%d" % dz):
            for dx in range(inner - 1, 0, -1):
                out = qx_out.at[dx - 1, dz], sx_out.at[dx - 1, dz]
                encode(functools.partial(pair_sum, dz, dx), *out)
                peer = (row_of(o, xs_of[dx], core), c)
                dst = qx.at[dx - 1, dz], sx.at[dx - 1, dz]
                post(out, dst, zx_sem.at[dx - 1, dz], peer, ALONG_X)

    def own_x():
        with scope("own_x"):
            landed(zc.at[pl.ds(0, outer)], zc_sem.at[0])

    def plane_sum(dz, t):
        total = pair_sum(dz, 0, t)
        for d in range(1, inner):
            total = total + decode(qx.at[d - 1, dz], sx.at[d - 1, dz], t)
        return total

    def arrived(d):
        landed(qz.at[d], zz_sem.at[d])

    def encode_z(dz, extra):
        def block(t):
            total = plane_sum(dz, t)
            for d in extra:
                total = total + decode(qz.at[d], sz.at[d], t)
            return total

        encode(block, qz_out.at[dz - 1], sz_out.at[dz - 1])

    def give_z(dz, extra=()):
        with scope("give_z%d" % dz):
            for d in range(1, inner):
                landed(qx.at[d - 1, dz], zx_sem.at[d - 1, dz])
            if dz == 0:
                for t in range(piece):
                    zs[t * vecs : (t + 1) * vecs] = plane_sum(0, t)
                return
            at, z = dz - 1, zs_of[dz]
            if merging and dz == 3:
                at, z = 3 - middle, zs_of[1] + middle * (zs_of[3] - zs_of[1])
            if extra:
                arrived(extra[0])
            encode_z(dz, extra)
            out = qz_out.at[dz - 1], sz_out.at[dz - 1]
            post(out, (qz.at[at], sz.at[at]), zz_sem.at[at], (row_of(z, i, core), c), ALONG_Z)

    def gram_plane(d, total):
        with scope("gram%d" % d):
            sums, mates = [], []
            for dx in range(inner):
                p = row_of(zs_of[d], xs_of[dx], core)
                for t in range(piece):
                    high, low = split(pair_sum(d, dx, t))
                    sums.append(jnp.concatenate([high, low], 0))
                    mates.append(cv[p * piece + t])
            return total + mul(jnp.concatenate(sums, 1), jnp.concatenate(mates, 1), across)

    def spread(value, buf, stage, me, far):
        with scope("spread%d" % stage):
            buf[me] = value
            for peer in far:
                send(buf.at[me], buf.at[me], g_sem.at[stage], peer, GRAM + stage)

    def collect(buf, stage):
        with scope("collect%d" % stage):
            landed(buf.at[pl.ds(0, buf.shape[0] - 1)], g_sem.at[stage])
            total = buf[0]
            for q in range(1, buf.shape[0]):
                total = total + buf[q]
            return total

    turn_tiles()
    with scope("wait_left"):
        for copy in own:
            copy.wait()
        for y in y_src:
            landed(rv_at(y), left_sem.at[y])

    def left_images(first, last):
        with scope("imgL%d" % first):
            images(first, last, tbuf, rv, row_s, block_rows)

    def right_images(first, last):
        with scope("imgR%d" % first):
            images(first, last, tflip, cv, col_s, block_cols)

    def maybe(step, d):
        if d < outer:
            step(d)

    left_images(0, 2)
    maybe(take_z, 1)
    left_images(2, chunks)
    take_x(0)
    pl.when(core == 1)(lambda: maybe(take_z, 2))
    with scope("gatherZa"):
        gather_sums(col_v, block_cols, zp, 0, vecs // 2)
    pl.when(core == 0)(lambda: maybe(take_z, 2))
    with scope("gatherZb"):
        gather_sums(col_v, block_cols, zp, vecs // 2, vecs)
    for d in range(3, outer):
        take_z(d)
    give_core()
    todo_x, todo_z = list(z_order), list(z_order)
    paired(todo_x[0])
    give_x(todo_x.pop(0))
    maybe(take_x, 1)
    for d in range(2, outer - 1):
        take_x(d)
    for d in todo_x:
        paired(d)
    while len(todo_x) > 2:
        give_x(todo_x.pop(0))
    own_x()
    total = jnp.zeros((2 * vecs, vecs), F32)
    for d in range(outer):
        if d == outer - 1 > 1:
            take_x(d)
        total = gram_plane(d, total)
    spread(total[:vecs] + total[vecs:], gb, 1, o * n_c + c, wide_peers)
    while len(todo_x) > 1:
        give_x(todo_x.pop(0))
    take_core()
    first = todo_z.pop(0)
    right_images(0, 2)
    give_z(first)
    give_x(todo_x.pop(0))
    right_images(2, chunks)

    def give_y(h):
        rows = vecs // HALVES
        with scope("gatherY%d" % h):
            gather_sums(row_v, block_rows, yp, h * rows, (h + 1) * rows)
        with scope("give_y%d" % h):
            for d, y in enumerate(y_far):
                out = qy_out.at[d, h], sy_out.at[d, h]
                start = y * part + h * rows
                encode(lambda t: yp[pl.ds(start + t * wide, rows), :], *out, rows)
                dst = qy.at[d, h], sy.at[d, h]
                post(out, dst, zy_sem.at[d, h], (r, y), ALONG_Y, rows)

    if merging:
        pl.when(middle == 0)(lambda: give_z(2))
        todo_z.remove(2)
    for h in range(HALVES):
        give_y(h)
    while len(todo_z) > 1:
        give_z(todo_z.pop(0))
    spread(collect(gb, 1), ga, 0, i * 2 + core, near_peers)
    if merging:
        pl.when(middle == 1)(lambda: give_z(2, [3]))
    give_z(0)
    gram = collect(ga, 0)
    with scope("correct"):
        gram = gram * (block_cols * n_c * side) ** (-0.5)
        out_g[...] = gram
        high, low = split(gram)
        turned_high, turned_low = split(gram.T)
        for t in range(piece):
            mine = cv[r * piece + t]
            out_y[t] = yp[pl.ds(c * part + t * wide, vecs), :] - (
                mul(turned_high, mine) + mul(turned_low, mine)
            )
            mine = rv[c * piece + t]
            out_z[t] = zs[t * vecs : (t + 1) * vecs] - (mul(high, mine) + mul(low, mine))
    for h in range(HALVES):
        rows = vecs // HALVES
        with scope("wait_y%d" % h):
            for d in range(n_c - 1):
                landed(qy.at[d, h], zy_sem.at[d, h])
        for t in range(piece):
            total = out_y[t, h * rows : (h + 1) * rows]
            for d in range(n_c - 1):
                total = total + decode(qy.at[d, h], sy.at[d, h], t, rows)
            out_y[t, h * rows : (h + 1) * rows] = total
    def add_z(slots_in):
        with scope("wait_z"):
            for d in slots_in:
                arrived(d)
        for t in range(piece):
            total = out_z[t]
            for d in slots_in:
                total = total + decode(qz.at[d], sz.at[d], t)
            out_z[t] = total

    if merging:
        pl.when(middle == 1)(lambda: add_z([0, 2, 1]))
        pl.when(middle == 0)(lambda: add_z([0, 1]))
    else:
        add_z(list(range(outer - 1)))
    with scope("wait_send"):
        left_here(cv.at[pl.ds(0, (n_r - 1) * piece)], RIGHT)
        left_here(rv.at[pl.ds(0, (n_c - 1) * piece)], LEFT)
        left_here(zc, PAIRED)
        left_here(qx_out, ALONG_X)
        left_here(qz_out, ALONG_Z)
        left_here(qy_out, ALONG_Y)
        left_here(ga.at[pl.ds(0, 2 * inner - 1)], GRAM)
        left_here(gb.at[pl.ds(0, outer * n_c - 1)], GRAM + 1)


def flush(*refs):
    sem = refs[-1]
    half = len(refs) // 2
    copies = [
        pltpu.make_async_copy(refs[q], refs[half + q], sem.at[q]) for q in range(half)
    ]
    for copy in copies:
        copy.start()
    for copy in copies:
        copy.wait()


def solution(mesh):
    n_r, n_c = mesh.shape["row"], mesh.shape["col"]
    half = n_r // 2
    inner = 1 << ((half.bit_length() - 1) // 2)
    outer = half // inner

    def per_device(tiles, tile_row, tile_col, right_vecs, left_vecs):
        slots, side = tiles.shape[2], tiles.shape[3]
        piece, vecs, _ = right_vecs.shape
        chunks = 8
        wide = vecs + PAD
        part = piece * wide
        block_rows, block_cols = piece * n_c, piece * n_r
        planes = outer * inner
        near, far, mates = max(inner - 1, 1), max(outer - 1, 1), max(n_c - 1, 1)
        rows = vecs // HALVES
        coded = [((piece * (vecs + 2), side), jnp.int16), ((piece, side), F32)]
        halved = [((piece * (rows + 2), side), jnp.int16), ((piece, side), F32)]
        vmem = pl.BlockSpec(memory_space=pltpu.VMEM)
        dma = pltpu.SemaphoreType.DMA
        shapes = [(piece, vecs, side), (piece, vecs, side), (vecs, vecs)]
        held = pl.pallas_call(
            functools.partial(kernel, (n_r, n_c, outer, inner, chunks)),
            out_shape=tuple(pltpu.VMEM(shape, F32) for shape in shapes),
            in_specs=[pl.BlockSpec(memory_space=pltpu.HBM)] * 5,
            out_specs=(vmem, vmem, vmem),
            scratch_shapes=[
                pltpu.VMEM((slots, side, side), BF16),
                pltpu.VMEM((slots, side, side), BF16),
                pltpu.VMEM((block_cols, vecs, side), BF16),
                pltpu.VMEM((block_rows, vecs, side), BF16),
                pltpu.VMEM((slots * wide, side), F32),
                pltpu.VMEM((block_cols * wide, side), F32),
                pltpu.VMEM((planes, part, side), F32),
                pltpu.VMEM((piece * vecs, side), F32),
                *[
                    pltpu.VMEM(lead + shape, kind)
                    for lead in [(near, outer)] * 2 + [(far,), (outer,)]
                    for shape, kind in coded
                ],
                pltpu.VMEM((block_rows * wide, side), F32),
                *[pltpu.VMEM((mates, HALVES) + shape, kind) for shape, kind in halved * 2],
                pltpu.VMEM((2 * inner, vecs, vecs), F32),
                pltpu.VMEM((outer * n_c, vecs, vecs), F32),
                *[pltpu.SMEM((1, slots), jnp.int32)] * 2,
                *[pltpu.VMEM((1, slots), jnp.int32)] * 2,
                dma((6,)),
                dma((TILE_COPIES,)),
                dma((GRAM + 2,)),
                dma((n_c,)),
                dma((outer * inner,)),
                dma((1,)),
                dma((1 + (inner - 1) * outer,)),
                dma((near, outer)),
                dma((outer,)),
                dma((mates, HALVES)),
                dma((2,)),
            ],
            compiler_params=pltpu.CompilerParams(
                collective_id=0, has_side_effects=True, vmem_limit_bytes=44 * 1024 * 1024
            ),
            name="arnoldi_step",
        )(
            *[
                pltpu.with_memory_space_constraint(x, pltpu.HBM)
                for x in (
                    tile_row.reshape(1, slots),
                    tile_col.reshape(1, slots),
                    right_vecs,
                    left_vecs,
                    tiles,
                )
            ]
        )
        held = [pltpu.with_memory_space_constraint(x, pltpu.VMEM) for x in held]
        return pl.pallas_call(
            flush,
            out_shape=tuple(jax.ShapeDtypeStruct(shape, F32) for shape in shapes),
            in_specs=[vmem] * len(shapes),
            out_specs=(pl.BlockSpec(memory_space=pl.ANY),) * len(shapes),
            scratch_shapes=[dma((len(shapes),))],
            name="flush",
        )(*held)

    placed = (
        P("row", "col", None, None, None),
        P("row", "col", None),
        P("row", "col", None),
        P(("row", "col"), None, None),
        P(("row", "col"), None, None),
    )
    return jax.shard_map(
        per_device,
        mesh=mesh,
        in_specs=placed,
        out_specs=(P(("row", "col"), None, None), P(("row", "col"), None, None), P()),
        check_vma=False,
    )
```
